32 devices in a mesh: grp: 8 (over z, core), tp: 4 (over y, x).
Axes of the slice: x: 2, y: 2, z: 4, core: 2. Of those that a mesh axis runs over, the one named last changes fastest.
Arguments:
- stream: bfloat16 [2048, 2048], P(('grp', 'tp')), may hold values from -6 to 6
- lengths: int32 [6], replicated, may hold values from 1 to 1024, 2048 in all
- att_routes: int32 [2048, 2], P(('grp', 'tp')), may hold values from 0 to 7, all different within a row
- att_gate: bfloat16 [2048, 2], P(('grp', 'tp')), may hold values from 0.19921875 to 1
- mlp_routes: int32 [2048, 2], P(('grp', 'tp')), may hold values from 0 to 7, all different within a row; in each aligned block of 256 rows (0 to 255, 256 to 511, ...) at most 80 rows name the same one
- mlp_gate: bfloat16 [2048, 2], P(('grp', 'tp')), may hold values from 0.19921875 to 1
- gain_attn: float32 [2048], replicated, may hold values from 0.25 to 1.75
- gain_mlp: float32 [2048], replicated, may hold values from 0.25 to 1.75
- w_query: bfloat16 [8, 2048, 2048], P(None, None, 'tp')
- w_key: bfloat16 [2048, 2048], P(None, 'tp')
- w_value: bfloat16 [2048, 2048], P(None, 'tp'), may hold values from -0.125 to 0.125
- w_output: bfloat16 [8, 2048, 2048], P(None, 'tp'), may hold values from -0.125 to 0.125
- w_gate: bfloat16 [2048, 45056], P(None, ('grp', 'tp')), may hold values from -0.125 to 0.125
- w_up: bfloat16 [2048, 45056], P(None, ('grp', 'tp')), may hold values from -0.125 to 0.125
- w_down: bfloat16 [45056, 2048], P(('grp', 'tp')), may hold values from -0.078125 to 0.078125
- cache_in: bfloat16 [2048, 4, 2, 16, 128], P('grp', None, None, 'tp'), may hold values from -6 to 6
- page_table: int32 [128], P('grp'), may hold values from 0 to 127, as said below
Outputs:
- hidden_out: bfloat16 [2048, 2048], P('grp', 'tp')
- cache_out: bfloat16 [128, 16, 4, 2, 16, 128], P('grp', None, None, None, 'tp')
The draws below stay inside these ranges and needn't reach their ends.
Inputs may be any that keep to these rules, and one draw needn't show every extreme that they name: Request r takes the lengths[r] tokens after those of requests 0 to r - 1; they sum to 2048 and the longest has exactly 1024. `att_routes`: the 2 experts of a token differ. `mlp_routes`: the 2 experts of a token differ; in each aligned block of 256 rows no expert is named by more than 80 rows, a bound that some block reaches. `page_table`: a permutation; of the 16 pages of each aligned block of 16 pages, exactly 2 go to each aligned block of 16 slots.
All inputs are finite; a program needn't handle non-finite values.
Results may differ from the reference program's by a relative error of at most 0.014.
Values may be sent and summed in bfloat16 or wider, within the bound.
A program may use at most 192 MiB of HBM per device.

```python
import math
import jax
import jax.numpy as jnp
import numpy as np
from jax import lax

D = 2048
HEADS = 16
HD = 128
E_ATT = 8
E_MLP = 8
FF = 5632
TOPK = 2
TOK_DEV = 256
REQS = 6
PAGE = 16
CLAYERS = 4
TOKENS = 2048
MOST_LEN = 1024
CAP = 80
PPD = 16
PAIR = 2
PAGES = 128
N_GRP = 8


def key_matrix(key):
    return jax.random.normal(jax.random.fold_in(key, 7), (D, HEADS * HD), jnp.float32) * D ** (-0.5)


def draw_w_key(key, part):
    return key_matrix(key).astype(jnp.bfloat16)


def draw_w_query(key, part):
    noise_part = jax.random.normal(jax.random.fold_in(key, 8), (E_ATT, D, HEADS * HD), jnp.float32) * D ** (-0.5)
    return noise_part.astype(jnp.bfloat16)


def draw_page_table(key, part):
    blocks = PAGES // PPD
    source_keys = jax.random.split(jax.random.fold_in(key, 21), blocks)
    page_ranks = jax.vmap(lambda sub_key: jax.random.permutation(sub_key, PPD))(source_keys)
    owner_block = page_ranks // PAIR
    within = page_ranks % PAIR
    owner_keys = jax.random.split(jax.random.fold_in(key, 22), blocks)
    owner_order = jax.vmap(lambda sub_key: jax.random.permutation(sub_key, PPD))(owner_keys)
    source = jnp.arange(blocks, dtype=jnp.int32)[:, None]
    local_slot = owner_order[owner_block, source * PAIR + within]
    return (owner_block * PPD + local_slot).reshape(-1).astype(jnp.int32)


def block_levels(stream_key, shape, cuts, least, top_value):
    loudness = 1.0
    for dim, blocks in cuts:
        heights = jax.random.uniform(jax.random.fold_in(jax.random.fold_in(stream_key, 6), dim), (blocks,), jnp.float32, least / len(cuts), top_value / len(cuts))
        loudness = loudness * jnp.repeat(jnp.exp(heights), shape[dim] // blocks).reshape((-1,) + (1,) * (len(shape) - 1 - dim))
    return loudness


def picks_of(rng, rows, count, top, lift):
    ranking = jax.random.permutation(jax.random.fold_in(rng, 1), count)
    favour = ranking
    for power in range(3):
        favour = favour * favour // count
    favour = favour * lift // count
    lots = jax.random.randint(jax.random.fold_in(rng, 2), (rows, count), 0, 4096) + favour
    holders = jax.random.permutation(jax.random.fold_in(rng, 3), rows)[jnp.arange(count) % rows]
    lots = jnp.where(jnp.arange(rows)[:, None] == holders[None, :], 1 << 14, lots)
    priority = lots * count + jnp.arange(count)
    return lax.top_k(priority.astype(jnp.int32), top)[1].astype(jnp.int32)


def length_profile(number_of, total, reach, slope):
    loads = [(1 << 20) // math.isqrt(standing ** slope) + 1 for standing in range(2, number_of + 1)]
    surplus, counts = total - reach - (number_of - 1), [1] * (number_of - 1)
    while surplus > 0:
        movable = [i for i in range(number_of - 1) if counts[i] < reach]
        pool, remaining = sum([loads[i] for i in movable]), surplus
        for i in movable:
            extra = min(reach - counts[i], max(1, remaining * loads[i] // pool), surplus)
            counts[i] = counts[i] + extra
            surplus = surplus - extra
    return np.array([reach] + counts)


def ragged_sizes(key, amount, total, reach, skew):
    if amount == 2:
        one = jax.random.randint(key, (), max(1, total - reach), min(reach, total - 1) + 1)
        return jnp.stack([one, total - one])
    sizes = jnp.asarray(length_profile(amount, total, reach, skew), jnp.int32)
    pairs = (amount - 1) // 2
    source_of, sink = sizes[1:1 + 2 * pairs:2], sizes[2:2 + 2 * pairs:2]
    margin = jnp.minimum(source_of - 1, reach - sink)
    moved = jax.random.randint(jax.random.fold_in(key, 1), (pairs,), 0, 1 << 20) % (margin + 1)
    sizes = sizes.at[1:1 + 2 * pairs:2].set(source_of - moved).at[2:2 + 2 * pairs:2].set(sink + moved)
    return sizes[jax.random.permutation(jax.random.fold_in(key, 2), amount)]


def deal_out(rng, own, number, rows, count, top, most, lean):
    order = jax.random.permutation(rng, count)
    packed, ordinary = shares(count, rows * top, most, lean, True), shares(count, rows * top, most, lean, False)
    places = jnp.arange(count)

    def named(sizes, rotation):
        used = int((sizes > 0).sum())
        fixed = max(1, used // 4)
        moved = fixed + (places - fixed + rotation * (used - fixed)) % max(1, count - fixed)
        return jnp.zeros((count,), jnp.int32).at[order[jnp.where(places < fixed, places, moved)]].set(jnp.asarray(sizes, jnp.int32))

    sizes = jnp.where(number % 4 == 0, named(packed, number // 4), named(ordinary, number - number // 4 - 1))
    mixed = jax.random.permutation(jax.random.fold_in(own, 3), count)
    source_of, taker = mixed[0:count // 2 * 2:2], mixed[1:count // 2 * 2:2]
    room = jnp.minimum(sizes[source_of] - 1, most - sizes[taker]) // 2
    room = jnp.where((source_of == order[0]) | (taker == order[0]) | (sizes[taker] == 0), 0, jnp.maximum(room, 0))
    moved = jax.random.randint(jax.random.fold_in(own, 4), (count // 2,), 0, 1 << 20) % (room + 1)
    sizes = sizes.at[source_of].add(-moved).at[taker].add(moved)
    labels = jnp.searchsorted(jnp.cumsum(sizes), jnp.arange(rows * top), side="right").astype(jnp.int32)
    grid = labels.reshape(top, rows).T
    grid = grid[jax.random.permutation(jax.random.fold_in(own, 1), rows)]
    rotation = jax.random.randint(jax.random.fold_in(own, 2), (rows, 1), 0, top)
    return jnp.take_along_axis(grid, (jnp.arange(top)[None, :] + rotation) % top, axis=1)


def shares(amount, total, bound, lean, full):
    portions = [(1 << 20) // math.isqrt(rank ** lean) + 1 for rank in range(1, amount + 1)]
    largest = bound if full else min(bound, max(-(-total // amount), total * portions[0] // sum(portions)))
    least = 1 if total - largest >= amount - 1 else 0
    given, rest = [largest] + [least] * (amount - 1), total - largest - least * (amount - 1)
    while rest > 0:
        candidates = [i for i in range(1, amount) if given[i] < largest] or [i for i in range(1, amount) if given[i] < bound]
        mass, left = sum([portions[i] for i in candidates]), rest
        for i in candidates:
            extra = min(bound - given[i], max(1, left * portions[i] // mass), rest)
            given[i] = given[i] + extra
            rest = rest - extra
    return np.array(given)


def noise(key, dims, deviation, reach, cuts=(), held_as=jnp.bfloat16):
    array = deviation * jax.random.normal(key, dims, jnp.float32)
    if cuts:
        array = array * block_levels(key, dims, cuts, -0.22, 0.18)
    return jnp.clip(array, -reach, reach).astype(held_as)


def setup_inputs(seed: int = 0) -> dict:
    key_list = jax.random.split(jax.random.key(seed), 18)
    stream = noise(key_list[0], (TOKENS, D), 1.0, 6.0, ((0, 32),))
    lengths = ragged_sizes(key_list[1], REQS, TOKENS, MOST_LEN, 2).astype(jnp.int32)
    att_routes = picks_of(key_list[2], TOKENS, E_ATT, TOPK, 2048)
    att_gate = jnp.clip(0.19921875 + 0.80078125 * jax.random.uniform(key_list[3], (TOKENS, TOPK), jnp.float32) ** block_levels(key_list[3], (TOKENS, TOPK), ((0, 32),), -0.2, 0.2), 0.19921875, 1.0).astype(jnp.bfloat16)
    mlp_routes_keys = jax.random.split(jax.random.fold_in(key_list[4], 1), TOKENS // TOK_DEV)
    mlp_routes_turns = jax.random.permutation(jax.random.fold_in(key_list[4], 3), TOKENS // TOK_DEV)
    mlp_routes = jax.vmap(lambda own, number: deal_out(jax.random.fold_in(key_list[4], 2), own, number, TOK_DEV, E_MLP, TOPK, CAP, 1))(mlp_routes_keys, mlp_routes_turns).reshape((TOKENS, TOPK))
    mlp_gate = jnp.clip(0.19921875 + 0.80078125 * jax.random.uniform(key_list[5], (TOKENS, TOPK), jnp.float32) ** block_levels(key_list[5], (TOKENS, TOPK), ((0, 32),), -0.2, 0.2), 0.19921875, 1.0).astype(jnp.bfloat16)
    gain_attn = jnp.clip(1.0 + 0.15 * jax.random.normal(key_list[6], (D,), jnp.float32), 0.25, 1.75)
    gain_mlp = jnp.clip(1.0 + 0.15 * jax.random.normal(key_list[7], (D,), jnp.float32), 0.25, 1.75)
    w_query = draw_w_query(jax.random.fold_in(key_list[17], 71), 0)
    w_key = draw_w_key(jax.random.fold_in(key_list[17], 71), 0)
    w_value = noise(key_list[10], (D, HEADS * HD), D ** -0.5, 0.125, ((1, 4),))
    w_output = noise(key_list[11], (E_ATT, HEADS * HD, D), (HEADS * HD) ** -0.5, 0.125, ((1, 4),))
    w_gate = noise(key_list[12], (D, E_MLP * FF), D ** -0.5, 0.125, ((1, 32),))
    w_up = noise(key_list[13], (D, E_MLP * FF), D ** -0.5, 0.125, ((1, 32),))
    w_down = noise(key_list[14], (E_MLP * FF, D), FF ** -0.5, 0.078125, ((0, 32),))
    cache_in = noise(key_list[15], (TOKENS, CLAYERS, 2, HEADS, HD), 1.0, 6.0, ((0, 8), (3, 4)))
    page_table = draw_page_table(jax.random.fold_in(key_list[17], 71), 0)
    return {"stream": stream, "lengths": lengths, "att_routes": att_routes, "att_gate": att_gate, "mlp_routes": mlp_routes, "mlp_gate": mlp_gate, "gain_attn": gain_attn, "gain_mlp": gain_mlp, "w_query": w_query, "w_key": w_key, "w_value": w_value, "w_output": w_output, "w_gate": w_gate, "w_up": w_up, "w_down": w_down, "cache_in": cache_in, "page_table": page_table}


epsilon = 1e-06
rope_base = 10000.0
masked_score = -1e+30

def rms_rows(row_values, gain_vector):
    widened = row_values.astype(jnp.float32)
    mean_square = lax.optimization_barrier(jnp.mean(widened * widened, axis=-1, keepdims=True))
    return (widened * lax.rsqrt(mean_square + epsilon) * gain_vector).astype(jnp.bfloat16)

def request_start(token_index, lengths):
    request_ends = jnp.cumsum(lengths, dtype=jnp.int32)
    passed = request_ends[None, :] <= token_index[:, None]
    starts = lax.optimization_barrier(jnp.max(jnp.where(passed, request_ends[None, :], 0), axis=1)).astype(jnp.int32)
    return (starts, lax.optimization_barrier(jnp.sum(passed.astype(jnp.int32), axis=1)).astype(jnp.int32))

def rope_turn(head_values, position):
    half_width = head_values.shape[-1] // 2
    frequency = rope_base ** (-(jnp.arange(half_width, dtype=jnp.float32) * 2.0 / head_values.shape[-1]))
    angles = position.astype(jnp.float32)[:, None] * frequency[None, :]
    view_shape = (angles.shape[0],) + (1,) * (head_values.ndim - 2) + (half_width,)
    cosine = jnp.cos(angles).reshape(view_shape)
    sine_part = jnp.sin(angles).reshape(view_shape)
    front_half = head_values[..., :half_width]
    back_half = head_values[..., half_width:]
    return jnp.concatenate([front_half * cosine - back_half * sine_part, back_half * cosine + front_half * sine_part], axis=-1)

def reference(stream, lengths, att_routes, att_gate, mlp_routes, mlp_gate, gain_attn, gain_mlp, w_query, w_key, w_value, w_output, w_gate, w_up, w_down, cache_in, page_table):
    token_index = jnp.arange(TOKENS, dtype=jnp.int32)
    starts, request = request_start(token_index, lengths)
    position = token_index - starts
    normed = rms_rows(stream, gain_attn)
    key_rows = rope_turn(jnp.dot(normed, w_key, preferred_element_type=jnp.float32).reshape(TOKENS, HEADS, HD), position).astype(jnp.bfloat16)
    value_rows = jnp.dot(normed, w_value, preferred_element_type=jnp.float32).reshape(TOKENS, HEADS, HD).astype(jnp.bfloat16)

    def add_query(running, expert):
        projected = jnp.dot(normed, w_query[expert], preferred_element_type=jnp.float32)
        hit_mask = (att_routes == expert).astype(jnp.float32)
        return (running + hit_mask[:, :, None] * projected[:, None, :], None)
    query_sum = lax.scan(add_query, jnp.zeros((TOKENS, TOPK, HEADS * HD), jnp.float32), jnp.arange(E_ATT, dtype=jnp.int32))[0]
    query_rows = rope_turn(query_sum.reshape(TOKENS, TOPK, HEADS, HD), position).astype(jnp.bfloat16)
    key_wide = lax.optimization_barrier(key_rows).astype(jnp.float32)
    value_wide = lax.optimization_barrier(value_rows).astype(jnp.float32)
    query_wide = lax.optimization_barrier(query_rows).astype(jnp.float32)
    query_block = math.gcd(TOKENS, 512)
    score_scale = HD ** (-0.5)

    def attend_block(first_row):
        query_part = lax.dynamic_slice_in_dim(query_wide, first_row, query_block, 0)
        row_index = first_row + jnp.arange(query_block, dtype=jnp.int32)
        row_request = lax.dynamic_slice_in_dim(request, first_row, query_block, 0)
        allowed = (request[None, :] == row_request[:, None]) & (token_index[None, :] <= row_index[:, None])
        scores = jnp.einsum('tkhd,shd->tkhs', query_part, key_wide) * score_scale
        live_pairs = allowed[:, None, None, :]
        scores = jnp.where(live_pairs, scores, masked_score)
        row_max = lax.optimization_barrier(jnp.max(scores, axis=-1, keepdims=True))
        weights = jnp.where(live_pairs, jnp.exp(scores - row_max), 0.0)
        rounded = lax.optimization_barrier(weights.astype(jnp.bfloat16)).astype(jnp.float32)
        return jnp.einsum('tkhs,shd->tkhd', rounded, value_wide) / lax.optimization_barrier(jnp.sum(weights, axis=-1))[..., None]
    attended = lax.map(attend_block, jnp.arange(0, TOKENS, query_block, dtype=jnp.int32)).reshape(TOKENS, TOPK, HEADS * HD)
    gate_wide = att_gate.astype(jnp.float32)

    def add_output(running, expert):
        mix_weight = jnp.where(att_routes == expert, gate_wide, 0.0)
        expert_mix = lax.optimization_barrier(jnp.sum(mix_weight[:, :, None] * attended, axis=1)).astype(jnp.bfloat16)
        return (running + jnp.dot(expert_mix, w_output[expert], preferred_element_type=jnp.float32), None)
    head_sum = lax.scan(add_output, jnp.zeros((TOKENS, D), jnp.float32), jnp.arange(E_ATT, dtype=jnp.int32))[0]
    middle = (stream.astype(jnp.float32) + head_sum).astype(jnp.bfloat16)
    normed_mid = rms_rows(middle, gain_mlp)
    limit = N_GRP * CAP
    mlp_wide = mlp_gate.astype(jnp.float32)

    def add_expert(running, expert):
        chosen = jnp.any(mlp_routes == expert, axis=1)
        weight = lax.optimization_barrier(jnp.sum(jnp.where(mlp_routes == expert, mlp_wide, 0.0), axis=1))
        picked_ids = jnp.nonzero(chosen, size=limit, fill_value=0)[0].astype(jnp.int32)
        valid_rows = jnp.arange(limit, dtype=jnp.int32) < jnp.sum(chosen.astype(jnp.int32))
        picked_rows = jnp.take(normed_mid, picked_ids, axis=0)
        gate_part = jnp.dot(picked_rows, lax.dynamic_slice_in_dim(w_gate, expert * FF, FF, 1), preferred_element_type=jnp.float32)
        up_part = jnp.dot(picked_rows, lax.dynamic_slice_in_dim(w_up, expert * FF, FF, 1), preferred_element_type=jnp.float32)
        hidden = (jax.nn.silu(gate_part) * up_part).astype(jnp.bfloat16)
        expert_out = jnp.dot(hidden, lax.dynamic_slice_in_dim(w_down, expert * FF, FF, 0), preferred_element_type=jnp.float32)
        scaled = jnp.where(valid_rows[:, None], jnp.take(weight, picked_ids)[:, None] * expert_out, 0.0)
        return (running.at[picked_ids].add(scaled), None)
    mlp_sum = lax.scan(add_expert, jnp.zeros((TOKENS, D), jnp.float32), jnp.arange(E_MLP, dtype=jnp.int32))[0]
    hidden_out = (middle.astype(jnp.float32) + mlp_sum).astype(jnp.bfloat16)
    page_blocks = cache_in.reshape(PAGES, PAGE, CLAYERS, 2, HEADS, HD)
    cache_out = jnp.zeros_like(page_blocks).at[page_table].set(page_blocks)
    return (hidden_out, cache_out)
```

```python
import functools
import types

import jax
import jax.numpy as jnp
from jax import lax
from jax.experimental import pallas as pl
from jax.experimental.pallas import tpu as pltpu
from jax.sharding import PartitionSpec as P

HD = 128
E_ATT = 8
E_MLP = 8
TOPK = 2
META = 128
STEP_BLOCKS = 2
MESH = pl.DeviceIdType.MESH
VMEM_LIMIT = 62 * 1024 * 1024


epsilon = 1e-06
rope_base = 10000.0
masked_score = -1e30

ANY = pl.BlockSpec(memory_space=pl.ANY)
VM = pl.BlockSpec(memory_space=pltpu.VMEM)
SM = pl.BlockSpec(memory_space=pltpu.SMEM)

bf16 = jnp.bfloat16
f32 = jnp.float32


def turn(part, cosine, sine):
    return part * cosine + pltpu.roll(part, HD // 2, 1) * sine


def eye(n):
    a = lax.broadcasted_iota(jnp.int32, (n, n), 0)
    return (a == lax.broadcasted_iota(jnp.int32, (n, n), 1)).astype(bf16)


def flip(values, size):
    return lax.dot_general(
        eye(size), values.astype(bf16), (((1,), (1,)), ((), ())), preferred_element_type=f32
    )


def page_scalars(table, count, pair):
    tokens = [table[i] for i in range(count)]
    owner = [lax.div(t, jnp.int32(count)) for t in tokens]
    place = []
    for i in range(count):
        rank = owner[i] * pair
        for j in range(i):
            rank = rank + jnp.where(owner[j] == owner[i], 1, 0)
        place.append(rank)
    order, local = [], []
    for d in range(count):
        at, slot = jnp.int32(0), jnp.int32(0)
        for i in range(count):
            hit = place[i] == d
            at = jnp.where(hit, i, at)
            slot = jnp.where(hit, tokens[i], slot)
        order.append(at)
        local.append(lax.rem(slot, jnp.int32(count)))
    return order, local


def layer_kernel(dims, names, *refs):
    (
        lengths, table, stream, att_routes, att_gate, mlp_routes, mlp_gate, gain_attn, gain_mlp, freq,
        w_query, w_key, w_value, w_out, w_gate, w_up, w_down, pages,
        hidden, arrived, slots,
    ) = refs[:21]
    b = types.SimpleNamespace(**dict(zip(names, refs[21:])))
    tp_count, grp_count, cap = dims
    tp = lax.axis_index("tp")
    grp = lax.axis_index("grp")
    core = grp % 2
    rows, model = stream.shape
    tok = rows * tp_count
    width = model // tp_count
    heads = width // HD
    hid = w_gate.shape[1]
    reach = grp_count // 2
    window = (reach + 1) * tok
    hops = reach // 2
    pages_dev = pages.shape[0]
    pair = pages_dev // grp_count
    peers = tp_count - 1
    square = tp_count == 4
    nx = tp + 1 - 2 * (tp % 2)
    ny = (tp + 2) % 4
    nd = 3 - tp

    def remote(src, dst, send, recv, peer):
        return pltpu.make_async_remote_copy(src, dst, send, recv, peer, MESH)

    def lanes_of(owner):
        return pl.ds(pl.multiple_of(owner * width, 128), width)

    def gather(block, whole, send, recv):
        if square:
            own = [
                remote(block(tp, 0), block(tp, 0), send.at[0], recv.at[0], {"tp": nx}),
                remote(block(tp, 1), block(tp, 1), send.at[2], recv.at[2], {"tp": ny}),
                remote(block(tp, 1), block(tp, 1), send.at[1], recv.at[1], {"tp": nx}),
                remote(block(tp, 0), block(tp, 0), send.at[3], recv.at[3], {"tp": ny}),
            ]
            on = [
                remote(block(nx, 0), block(nx, 0), send.at[4], recv.at[4], {"tp": ny}),
                remote(block(ny, 1), block(ny, 1), send.at[5], recv.at[5], {"tp": nx}),
            ]
        else:
            own = [
                remote(
                    whole(tp), whole(tp), send.at[j - 1], recv.at[j - 1],
                    {"tp": (tp + j) % tp_count},
                )
                for j in range(1, tp_count)
            ]
            on = []

        def start():
            for copy in own:
                copy.start()

        def forward():
            for first, copy in zip(own, on):
                first.wait_recv()
                copy.start()

        def finish():
            for copy in own[len(on):] + on:
                copy.wait_recv()

        def drain():
            for copy in own + on:
                copy.wait_send()

        return types.SimpleNamespace(start=start, forward=forward, finish=finish, drain=drain)

    def scatter(count, base, p_out, p_in, s_out, s_in, send, recv):
        half = count // 2
        upper, lower = pl.ds(base, half), pl.ds(base + half, half)
        if square:
            kx = remote(
                p_out.at[pl.ds(0, 2)], p_in.at[pl.ds(0, 2)], send.at[0], recv.at[0], {"tp": nx}
            )
            ky = remote(
                p_out.at[pl.ds(2, 2)], p_in.at[pl.ds(2, 2)], send.at[1], recv.at[1], {"tp": ny}
            )
            k2 = remote(s_out.at[0], s_in.at[0], send.at[2], recv.at[2], {"tp": ny})
            k3 = remote(s_out.at[1], s_in.at[1], send.at[3], recv.at[3], {"tp": nx})
            copies = [kx, ky, k2, k3]
        else:
            copies = [
                remote(
                    p_out.at[j - 1], p_in.at[j - 1], send.at[j - 1], recv.at[j - 1],
                    {"tp": (tp + j) % tp_count},
                )
                for j in range(1, tp_count)
            ]

        def emit(part):
            if square:
                far = part(nd)
                p_out[1] = far[:half].astype(bf16)
                p_out[3] = far[half:].astype(bf16)
                side = part(nx)
                p_out[0] = side[:half].astype(bf16)
                kx.start()
                b.acc[lower, lanes_of(nx)] = side[half:]
                side = part(ny)
                p_out[2] = side[half:].astype(bf16)
                ky.start()
                b.acc[upper, lanes_of(ny)] = side[:half]
            else:
                for j in range(1, tp_count):
                    p_out[j - 1] = part((tp + j) % tp_count).astype(bf16)
                    copies[j - 1].start()
            b.acc[pl.ds(base, count), lanes_of(tp)] = part(tp)

        def middle():
            if square:
                kx.wait_recv()
                s_out[0] = (b.acc[upper, lanes_of(ny)] + p_in[1].astype(f32)).astype(bf16)
                k2.start()
                ky.wait_recv()
                s_out[1] = (b.acc[lower, lanes_of(nx)] + p_in[3].astype(f32)).astype(bf16)
                k3.start()

        def result():
            top, low = b.acc[upper, lanes_of(tp)], b.acc[lower, lanes_of(tp)]
            if square:
                k2.wait_recv()
                k3.wait_recv()
                top = top + p_in[0].astype(f32) + s_in[0].astype(f32)
                low = low + p_in[2].astype(f32) + s_in[1].astype(f32)
            else:
                for j, copy in enumerate(copies):
                    copy.wait_recv()
                    top = top + p_in[j, 0:half].astype(f32)
                    low = low + p_in[j, half:count].astype(f32)
            return top, low

        def drain():
            for copy in copies:
                copy.wait_send()

        return types.SimpleNamespace(emit=emit, middle=middle, result=result, drain=drain)

    load_pages = pltpu.make_async_copy(pages, b.held, b.page_sem.at[0])
    load_pages.start()
    load_k = pltpu.make_async_copy(w_key, b.wkv.at[:, pl.ds(0, width)], b.kv_sem.at[0])
    load_v = pltpu.make_async_copy(w_value, b.wkv.at[:, pl.ds(width, width)], b.kv_sem.at[1])
    load_k.start()
    load_v.start()
    room = min(E_ATT, b.wide.shape[1] // width)
    load_q = [
        pltpu.make_async_copy(
            w_query.at[e], b.wide.at[:, pl.ds((e % room) * width, width)], b.q_sem.at[e]
        )
        for e in range(E_ATT)
    ]
    for load in load_q[:room]:
        load.start()
    load_o = [
        [
            pltpu.make_async_copy(
                w_out.at[e, pl.ds(h * HD, HD)], b.wo.at[h, pl.ds(e * HD, HD)], b.o_sem.at[h, e]
            )
            for e in range(E_ATT)
        ]
        for h in range(heads)
    ]

    barrier = pltpu.get_barrier_semaphore()
    for j in range(1, tp_count):
        pl.semaphore_signal(
            barrier, inc=1, device_id={"tp": (tp + j) % tp_count}, device_id_type=MESH
        )
    for j in range(1, grp_count):
        pl.semaphore_signal(
            barrier, inc=1, device_id={"grp": (grp + j) % grp_count}, device_id_type=MESH
        )

    mine = pl.ds(pl.multiple_of(tp * rows, rows), rows)
    b.rows_all[mine, :] = stream[...]
    fields = [
        ref[...].astype(f32) for ref in (att_routes, att_gate, mlp_routes, mlp_gate)
    ]
    fields = jnp.concatenate(fields + [jnp.zeros((META - 4 * TOPK, rows), f32)], axis=0)
    b.info[mine, :] = flip(fields, rows).astype(bf16)
    pl.semaphore_wait(barrier, tp_count - 1 + grp_count - 1)

    def row_block(owner, half):
        size = rows // 2
        return b.rows_all.at[pl.ds(pl.multiple_of(owner * rows + half * size, 16), size)]

    def row_whole(owner):
        return b.rows_all.at[pl.ds(pl.multiple_of(owner * rows, rows), rows)]

    rows_gather = gather(row_block, row_whole, b.row_send, b.row_recv)
    rows_gather.start()
    info_copies = [
        remote(
            b.info.at[mine], b.info.at[mine], b.info_send.at[j - 1], b.info_recv.at[j - 1],
            {"tp": (tp + j) % tp_count},
        )
        for j in range(1, tp_count)
    ]
    for copy in info_copies:
        copy.start()

    order, local = page_scalars(table, pages_dev, pair)
    lane = lax.broadcasted_iota(jnp.int32, (1, META), 1)
    for p in range(grp_count):
        line = jnp.zeros((1, META), jnp.int32)
        for n in range(pair):
            line = jnp.where(lane == n, local[p * pair + n], line)
        b.slot_out[p] = line
    load_pages.wait()
    for load in [x for line in load_o for x in line]:
        load.start()
    page_copies = []

    def pick_pages(n):
        for p in range(grp_count):
            for half in range(2):
                b.staged[n, half, p] = b.held[order[p * pair + n], half]

    def send_pages(turn_index):
        n, half = turn_index // 2, turn_index % 2
        keep = pltpu.make_async_copy(
            b.staged.at[n, half, grp], arrived.at[grp, n, half], b.self_sem.at[turn_index]
        )
        keep.start()
        page_copies.append(keep)
        for j in range(1, grp_count):
            peer = (grp + j) % grp_count
            copy = remote(
                b.staged.at[n, half, peer], arrived.at[grp, n, half],
                b.page_send.at[turn_index, j - 1], b.page_recv.at[turn_index, j - 1],
                {"grp": peer},
            )
            copy.start()
            page_copies.append(copy)

    pick_pages(0)
    send_pages(0)
    rows_gather.forward()
    for n in range(1, pair):
        pick_pages(n)
    slots[grp] = b.slot_out[grp]
    for j in range(1, grp_count):
        peer = (grp + j) % grp_count
        copy = remote(
            b.slot_out.at[peer], slots.at[grp], b.slot_send.at[j - 1], b.slot_recv.at[j - 1],
            {"grp": peer},
        )
        copy.start()
        page_copies.append(copy)

    index = lax.broadcasted_iota(jnp.int32, (tok, 1), 0) + grp * tok
    starts = jnp.zeros((tok, 1), jnp.int32)
    end = jnp.int32(0)
    for r in range(lengths.shape[0]):
        end = end + lengths[r]
        starts = jnp.where(index >= end, end, starts)
    angles = (index - starts).astype(f32) * freq[...]
    b.cosine[...] = jnp.cos(angles)
    sign = jnp.where(lax.broadcasted_iota(jnp.int32, (1, HD), 1) < HD // 2, -1.0, 1.0)
    b.sine[...] = jnp.sin(angles) * sign
    column = lax.broadcasted_iota(jnp.int32, (tok, window), 1) + (grp - reach) * tok
    b.bias[...] = jnp.where((column <= index) & (column >= starts), 0.0, masked_score)

    rows_gather.finish()
    widened = b.rows_all[...].astype(f32)
    mean_square = jnp.mean(widened * widened, axis=-1, keepdims=True)
    b.normed[...] = (widened * lax.rsqrt(mean_square + epsilon) * gain_attn[...]).astype(bf16)
    b.mid[...] = b.rows_all[:, lanes_of(tp)]

    onward = {"grp": (grp + 2) % grp_count}
    other = {"grp": grp + 1 - 2 * core}
    rings = [
        [
            remote(
                b.kv.at[h, reach - 2 * n], b.kv.at[h, reach - 2 * n - 2],
                b.ring_send.at[h, n], b.ring_recv.at[h, n], onward,
            )
            for n in range(hops)
        ]
        for h in range(heads)
    ]
    sides = [
        [
            remote(
                b.kv.at[h, reach - 2 * (core + n)], b.kv.at[h, reach - 1 - 2 * n],
                b.side_send.at[h, n], b.side_recv.at[h, n], other,
            )
            for n in range(hops)
        ]
        for h in range(heads)
    ]
    load_k.wait()
    load_v.wait()
    for two in range(heads // 2):
        at = two * 2 * HD
        keys = jnp.dot(b.normed[...], b.wkv[:, at : at + 2 * HD], preferred_element_type=f32)
        values = jnp.dot(
            b.normed[...], b.wkv[:, width + at : width + at + 2 * HD], preferred_element_type=f32
        )
        for i in range(2):
            part = slice(i * HD, (i + 1) * HD)
            h = 2 * two + i
            b.kv[h, reach, :, :HD] = turn(keys[:, part], b.cosine[...], b.sine[...]).astype(bf16)
            b.kv[h, reach, :, HD:] = values[:, part].astype(bf16)
            rings[h][0].start()

    for copy in info_copies:
        copy.wait_recv()
    ids = b.info[...].astype(f32)

    def project(e):
        load_q[e].wait()
        at = (e % room) * width
        projected = jnp.dot(b.normed[...], b.wide[:, at : at + width], preferred_element_type=f32)
        if e + room < E_ATT:
            load_q[e + room].start()
        for k in range(TOPK):
            total = b.acc[:tok, k * width : (k + 1) * width] if e else 0.0
            b.acc[:tok, k * width : (k + 1) * width] = jnp.where(
                ids[:, k : k + 1] == float(e), projected, total
            )

    share = E_ATT // heads
    for n in range(hops - 1):
        for h in range(heads):
            if n == 0:
                for e in range(h * share, (h + 1) * share):
                    project(e)
            rings[h][n].wait_recv()
            rings[h][n + 1].start()
            sides[h][n].start()
    wide_loads = [
        pltpu.make_async_copy(w_gate, b.wg, b.w_sem.at[0])
        if hasattr(b, "wg")
        else pltpu.make_async_copy(w_gate, b.wide.at[:, pl.ds(0, hid)], b.w_sem.at[0]),
        pltpu.make_async_copy(w_up, b.wu, b.w_sem.at[1])
        if hasattr(b, "wu")
        else pltpu.make_async_copy(w_up, b.wide.at[:, pl.ds(hid, hid)], b.w_sem.at[1]),
    ]
    for load in wide_loads:
        load.start()
    for k in range(TOPK):
        for h in range(heads):
            at = k * width + h * HD
            b.query[k, h] = turn(
                b.acc[:tok, at : at + HD], b.cosine[...], b.sine[...]
            ).astype(bf16)

    across = lax.dot_general(
        eye(META), ids.astype(bf16), (((1,), (1,)), ((), ())), preferred_element_type=f32
    )
    lower_mask = (
        lax.broadcasted_iota(jnp.int32, (tok, tok), 0)
        < lax.broadcasted_iota(jnp.int32, (tok, tok), 1)
    ).astype(bf16)
    at = 2 * TOPK
    hits, weigh = [], []
    for e in range(E_MLP):
        hot = [across[at + k : at + k + 1, :] == float(e) for k in range(TOPK)]
        gates = [
            jnp.where(hot[k], across[at + TOPK + k : at + TOPK + k + 1, :], 0.0)
            for k in range(TOPK)
        ]
        weigh.append(gates[0] + gates[1])
        hits.append(jnp.where(hot[0] | hot[1], 1.0, 0.0))
    hit = jnp.concatenate(hits, axis=0)
    rank = jnp.dot(hit.astype(bf16), lower_mask, preferred_element_type=f32)
    rank = jnp.where(hit > 0.5, rank, -1.0)
    slot_ids = lax.broadcasted_iota(jnp.int32, (cap, tok), 0).astype(f32)
    per_owner = grp_count // E_MLP
    for e in range(E_MLP):
        placed = rank[e : e + 1, :] == slot_ids
        b.select[e * cap : (e + 1) * cap, :] = jnp.where(placed, 1.0, 0.0).astype(bf16)
        value = jnp.where(placed, weigh[e], 0.0).astype(bf16)
        for i in range(per_owner):
            g = e * per_owner + i
            b.mix[g * cap : (g + 1) * cap, :] = value

    scale = HD ** (-0.5)
    down_rows = E_ATT * HD
    down_parts = [
        (c, min(down_rows, hid - c * down_rows)) for c in range(-(-hid // down_rows))
    ]
    down_loads = [
        pltpu.make_async_copy(
            w_down.at[pl.ds(c * down_rows, size)], b.wo.at[c, pl.ds(0, size)], b.w_sem.at[2 + c]
        )
        for c, size in down_parts
    ]

    def ready(h):
        rings[h][hops - 1].wait_recv()
        sides[h][hops - 1].start()

    rounds = pair * 2
    ready(0)
    out_scatter = scatter(tok, 0, b.po2, b.pi2, b.so2, b.si2, b.s2_send, b.s2_recv)
    for h in range(heads):
        for n in range(hops):
            sides[h][n].wait_recv()
        key_head = b.kv[h, :, :, :HD].reshape(window, HD)
        value_head = b.kv[h, :, :, HD:].reshape(window, HD)
        att = []
        for k in range(TOPK):
            scores = lax.dot_general(
                b.query[k, h], key_head, (((1,), (1,)), ((), ())), preferred_element_type=f32
            ) + b.bias[...]
            top = jnp.max(scores, axis=-1, keepdims=True)
            weights = jnp.exp((scores - top) * scale)
            weight_sum = jnp.sum(weights, axis=-1, keepdims=True)
            summed = jnp.dot(weights.astype(bf16), value_head, preferred_element_type=f32)
            att.append(summed / weight_sum)
        if h + 1 < heads:
            ready(h + 1)
        else:
            for i in range(1, rounds - 1):
                send_pages(i)
        for e in range(E_ATT):
            mixed = None
            for k in range(TOPK):
                gate = jnp.where(
                    ids[:, k : k + 1] == float(e), ids[:, TOPK + k : TOPK + k + 1], 0.0
                )
                term = gate * att[k]
                mixed = term if mixed is None else mixed + term
            b.normed[:, e * HD : (e + 1) * HD] = mixed.astype(bf16)
        for load in load_o[h]:
            load.wait()
        if h + 1 < heads:
            for j in range(tp_count):
                lanes = slice(j * width, (j + 1) * width)
                part = jnp.dot(
                    b.normed[:, :down_rows], b.wo[h, :, lanes], preferred_element_type=f32
                )
                b.acc[:tok, lanes] = part if h == 0 else b.acc[:tok, lanes] + part
            if h < len(down_loads):
                down_loads[h].start()
        else:

            def last_part(owner):
                return b.acc[:tok, lanes_of(owner)] + jnp.dot(
                    b.normed[:, :down_rows], b.wo[h, :, lanes_of(owner)],
                    preferred_element_type=f32,
                )

            out_scatter.emit(last_part)
    out_scatter.middle()
    top, low = out_scatter.result()
    half = tok // 2
    b.mid[:half, :] = (b.mid[:half, :].astype(f32) + top).astype(bf16)
    b.mid[half:, :] = (b.mid[half:, :].astype(f32) + low).astype(bf16)

    rows_gather.drain()

    step_rows = STEP_BLOCKS * cap
    steps = grp_count // STEP_BLOCKS
    for e in range(E_MLP):
        b.picked[e] = jnp.dot(
            b.select[e * cap : (e + 1) * cap, :], b.mid[...], preferred_element_type=f32
        ).astype(bf16)
    dispatch = []
    for i in range(1, grp_count):
        peer = (grp + grp_count - i) % grp_count
        copy = remote(
            b.picked.at[peer // per_owner], b.gathered.at[tp, pl.ds(i * cap, cap)],
            b.d_send.at[i - 1], b.d_recv.at[i - 1], {"grp": peer},
        )
        copy.start()
        dispatch.append(copy)
    b.gathered[tp, 0:cap, :] = b.picked[grp // per_owner]

    def step_gather(step):
        def block(owner, half):
            return b.gathered.at[owner, pl.ds((STEP_BLOCKS * step + half) * cap, cap)]

        def whole(owner):
            return b.gathered.at[owner, pl.ds(step * step_rows, step_rows)]

        return gather(block, whole, b.g_send.at[step], b.g_recv.at[step])

    gathers = [step_gather(s) for s in range(steps)]
    scatters = [
        scatter(
            step_rows, (s % 2) * step_rows, b.po3.at[s], b.pi3.at[s], b.so3.at[s], b.si3.at[s],
            b.s3_send.at[s], b.s3_recv.at[s],
        )
        for s in range(steps)
    ]

    def pass_on(step):
        for i in range(step * STEP_BLOCKS, (step + 1) * STEP_BLOCKS):
            if i:
                dispatch[i - 1].wait_recv()
        gathers[step].start()

    ret = []

    def give_back(step):
        for q, value in enumerate(scatters[step].result()):
            i = step * STEP_BLOCKS + q
            back = pl.ds(pl.multiple_of(grp * cap, cap), cap)
            if i == 0:
                b.ret_in[back, :] = value.astype(bf16)
            else:
                b.ret_out[i * cap : (i + 1) * cap, :] = value.astype(bf16)
                copy = remote(
                    b.ret_out.at[pl.ds(i * cap, cap)], b.ret_in.at[back],
                    b.t_send.at[i - 1], b.t_recv.at[i - 1], {"grp": (grp + i) % grp_count},
                )
                copy.start()
                ret.append(copy)

    pass_on(0)
    pass_on(1)
    gathers[0].forward()
    for load in wide_loads + down_loads:
        load.wait()
    for step in range(steps):
        part = slice(step * step_rows, (step + 1) * step_rows)
        gathers[step].finish()
        if step + 2 < steps:
            pass_on(step + 2)
        if step + 1 < steps:
            gathers[step + 1].forward()
        if step + 3 == steps:
            send_pages(rounds - 1)
        square_sum = None
        for s in range(tp_count):
            block = b.gathered[s, part, :].astype(f32)
            term = jnp.sum(block * block, axis=-1, keepdims=True)
            square_sum = term if square_sum is None else square_sum + term
        factor = lax.rsqrt(square_sum * (1.0 / model) + epsilon)
        for s in range(tp_count):
            lanes = slice(s * width, (s + 1) * width)
            b.rows_all[:step_rows, lanes] = (
                b.gathered[s, part, :].astype(f32) * factor * gain_mlp[:, lanes]
            ).astype(bf16)
        xn = b.rows_all[:step_rows, :]
        wg = b.wg[...] if hasattr(b, "wg") else b.wide[:, :hid]
        wu = b.wu[...] if hasattr(b, "wu") else b.wide[:, hid : 2 * hid]
        gate = jnp.dot(xn, wg, preferred_element_type=f32)
        up = jnp.dot(xn, wu, preferred_element_type=f32)
        units = (gate / (1.0 + jnp.exp(-gate)) * up).astype(bf16)
        if step >= 1:
            scatters[step - 1].middle()
        if step >= 2:
            give_back(step - 2)

        def down(owner):
            total = None
            for c, size in down_parts:
                term = jnp.dot(
                    units[:, c * down_rows : c * down_rows + size],
                    b.wo[c, :size, lanes_of(owner)], preferred_element_type=f32,
                )
                total = term if total is None else total + term
            return total

        scatters[step].emit(down)
    if steps >= 2:
        give_back(steps - 2)
    scatters[steps - 1].middle()
    give_back(steps - 1)
    for copy in ret:
        copy.wait_recv()
    hidden[...] = (
        b.mid[...].astype(f32)
        + lax.dot_general(
            b.mix[...], b.ret_in[...], (((0,), (0,)), ((), ())), preferred_element_type=f32
        )
    ).astype(bf16)
    for copy in page_copies:
        copy.wait()
    for copy in info_copies + dispatch + ret + [x for line in rings + sides for x in line]:
        copy.wait_send()
    for group in [out_scatter] + gathers + scatters:
        group.drain()


def place_kernel(slot_of, arrived, layer_out, placed, hidden_out, sem, out_sem):
    copies = [pltpu.make_async_copy(layer_out, hidden_out, out_sem.at[0])]
    groups, pair = arrived.shape[:2]
    for g in range(groups):
        for n in range(pair):
            copies.append(
                pltpu.make_async_copy(
                    arrived.at[g, n], placed.at[slot_of[g, 0, n]], sem.at[g * pair + n]
                )
            )
    for copy in copies:
        copy.start()
    for copy in copies:
        copy.wait()


def on_device(
    stream,
    lengths,
    att_routes,
    att_gate,
    mlp_routes,
    mlp_gate,
    gain_attn,
    gain_mlp,
    w_query,
    w_key,
    w_value,
    w_output,
    w_gate,
    w_up,
    w_down,
    cache_in,
    page_table,
):
    grp_count = lax.axis_size("grp")
    tp_count = lax.axis_size("tp")
    rows, model = stream.shape
    tok = rows * tp_count
    width = w_key.shape[1]
    heads = width // HD
    hid = w_gate.shape[1]
    pages_dev = page_table.shape[0]
    pair = pages_dev // grp_count
    dma = pltpu.SemaphoreType.DMA
    sds = jax.ShapeDtypeStruct
    vmem = pltpu.VMEM
    peers = tp_count - 1
    square = tp_count == 4
    cap = tok * TOPK * 5 // (E_MLP * 4)
    reach = grp_count // 2
    hops = reach // 2
    window = (reach + 1) * tok
    step_rows = STEP_BLOCKS * cap
    steps = grp_count // STEP_BLOCKS
    slots = grp_count * cap
    rounds = pair * 2

    frequency = rope_base ** (-(jnp.arange(HD // 2, dtype=f32) * 2.0 / HD))
    freq = jnp.concatenate([frequency, frequency])[None, :]
    page_len = tok // pages_dev
    piece = (page_len // 2 * cache_in.shape[1] * cache_in.shape[2],) + cache_in.shape[3:]
    pages = cache_in.reshape((pages_dev, 2) + piece)

    scratch = {
        "held": vmem((pages_dev, 2) + piece, bf16),
        "staged": vmem((pair, 2, grp_count) + piece, bf16),
        "slot_out": vmem((grp_count, 1, META), jnp.int32),
        "wkv": vmem((model, 2 * width), bf16),
        "wo": vmem((heads, E_ATT * HD, model), bf16),
        "rows_all": vmem((max(tok, step_rows), model), bf16),
        "normed": vmem((tok, model), bf16),
        "info": vmem((tok, META), bf16),
        "cosine": vmem((tok, HD), f32),
        "sine": vmem((tok, HD), f32),
        "bias": vmem((tok, window), f32),
        "kv": vmem((heads, reach + 1, tok, 2 * HD), bf16),
        "query": vmem((TOPK, heads, tok, HD), bf16),
        "acc": vmem((max(tok, 2 * step_rows), model), f32),
        "mid": vmem((tok, width), bf16),
        "select": vmem((E_MLP * cap, tok), bf16),
        "mix": vmem((slots, tok), bf16),
        "picked": vmem((E_MLP, cap, width), bf16),
        "gathered": vmem((tp_count, slots, width), bf16),
        "ret_out": vmem((slots, width), bf16),
        "ret_in": vmem((slots, width), bf16),
        "page_sem": dma((1,)),
        "kv_sem": dma((2,)),
        "q_sem": dma((E_ATT,)),
        "o_sem": dma((heads, E_ATT)),
        "w_sem": dma((2 + heads,)),
        "row_send": dma((max(6, peers),)),
        "row_recv": dma((max(6, peers),)),
        "info_send": dma((peers,)),
        "info_recv": dma((peers,)),
        "self_sem": dma((rounds,)),
        "page_send": dma((rounds, grp_count - 1)),
        "page_recv": dma((rounds, grp_count - 1)),
        "slot_send": dma((grp_count - 1,)),
        "slot_recv": dma((grp_count - 1,)),
        "ring_send": dma((heads, hops)),
        "ring_recv": dma((heads, hops)),
        "side_send": dma((heads, hops)),
        "side_recv": dma((heads, hops)),
        "s2_send": dma((max(4, peers),)),
        "s2_recv": dma((max(4, peers),)),
        "d_send": dma((grp_count - 1,)),
        "d_recv": dma((grp_count - 1,)),
        "g_send": dma((steps, max(6, peers))),
        "g_recv": dma((steps, max(6, peers))),
        "s3_send": dma((steps, max(4, peers))),
        "s3_recv": dma((steps, max(4, peers))),
        "t_send": dma((grp_count - 1,)),
        "t_recv": dma((grp_count - 1,)),
    }
    if hid % 128 == 0:
        scratch["wide"] = vmem((model, 2 * hid), bf16)
    else:
        scratch["wide"] = vmem((model, E_ATT * width), bf16)
        scratch["wg"] = vmem((model, hid), bf16)
        scratch["wu"] = vmem((model, hid), bf16)
    for stage, lead, count in (("2", (), tok), ("3", (steps,), step_rows)):
        if square:
            part, second = lead + (4, count // 2, width), lead + (2, count // 2, width)
        else:
            part, second = lead + (peers, count, width), lead + (1, 16, 128)
        scratch["po" + stage] = vmem(part, bf16)
        scratch["pi" + stage] = vmem(part, bf16)
        scratch["so" + stage] = vmem(second, bf16)
        scratch["si" + stage] = vmem(second, bf16)

    layer_out, arrived, slot_of = pl.pallas_call(
        functools.partial(layer_kernel, (tp_count, grp_count, cap), tuple(scratch)),
        out_shape=(
            sds((tok, width), bf16),
            sds((grp_count, pair, 2) + piece, bf16),
            sds((grp_count, 1, META), jnp.int32),
        ),
        in_specs=[SM] * 2 + [VM] * 8 + [ANY] * 8,
        out_specs=(VM, ANY, VM),
        scratch_shapes=list(scratch.values()),
        compiler_params=pltpu.CompilerParams(
            vmem_limit_bytes=VMEM_LIMIT, collective_id=1, has_side_effects=True
        ),
        name="layer",
    )(
        lengths, page_table, stream, att_routes.T, att_gate.T, mlp_routes.T, mlp_gate.T,
        gain_attn[None, :], gain_mlp[None, :], freq,
        w_query, w_key, w_value, w_output, w_gate, w_up, w_down, pages,
    )

    cache_out, hidden_out = pl.pallas_call(
        place_kernel,
        out_shape=(sds((pages_dev, 2) + piece, bf16), sds((tok, width), bf16)),
        in_specs=[SM, ANY, ANY],
        out_specs=(ANY, ANY),
        scratch_shapes=[dma((pages_dev,)), dma((1,))],
        compiler_params=pltpu.CompilerParams(vmem_limit_bytes=VMEM_LIMIT),
        name="place_pages",
    )(slot_of, arrived, layer_out)
    return (hidden_out, cache_out.reshape((pages_dev, page_len) + cache_in.shape[1:]))


def solution(mesh):
    return jax.shard_map(
        on_device,
        mesh=mesh,
        in_specs=(
            P(("grp", "tp"), None),
            P(),
            P(("grp", "tp"), None),
            P(("grp", "tp"), None),
            P(("grp", "tp"), None),
            P(("grp", "tp"), None),
            P(),
            P(),
            P(None, None, "tp"),
            P(None, "tp"),
            P(None, "tp"),
            P(None, "tp", None),
            P(None, ("grp", "tp")),
            P(None, ("grp", "tp")),
            P(("grp", "tp"), None),
            P("grp", None, None, "tp", None),
            P("grp"),
        ),
        out_specs=(P("grp", "tp"), P("grp", None, None, None, "tp", None)),
        check_vma=False,
    )
```

```python
import contextlib
import functools
import types

import jax
import jax.numpy as jnp
import numpy as np
from jax import lax
from jax.experimental import pallas as pl
from jax.experimental.pallas import tpu as pltpu
from jax.sharding import PartitionSpec as P

HD = 128
E_ATT = 8
E_MLP = 8
TOPK = 2
META = 128
STEP_BLOCKS = 2
PIECES = 4
WHEN = {"early": (8, 1), "kv": (0, 3), "out": (0, 0), "disp": (0, 4)}
MESH = pl.DeviceIdType.MESH
VMEM_LIMIT = 62 * 1024 * 1024
TRACE = False


epsilon = 1e-06
rope_base = 10000.0
masked_score = -1e30

ANY = pl.BlockSpec(memory_space=pl.ANY)
VM = pl.BlockSpec(memory_space=pltpu.VMEM)
SM = pl.BlockSpec(memory_space=pltpu.SMEM)

bf16 = jnp.bfloat16
f32 = jnp.float32


def scope(name):
    return jax.named_scope(name) if TRACE else contextlib.nullcontext()


def turn(part, cosine, sine):
    return part * cosine + pltpu.roll(part, HD // 2, 1) * sine


def eye(n):
    a = lax.broadcasted_iota(jnp.int32, (n, n), 0)
    return (a == lax.broadcasted_iota(jnp.int32, (n, n), 1)).astype(bf16)


def flip(values, size):
    return lax.dot_general(
        eye(size), values.astype(bf16), (((1,), (1,)), ((), ())), preferred_element_type=f32
    )


def page_scalars(table, count, pair):
    tokens = [table[i] for i in range(count)]
    owner = [lax.div(t, jnp.int32(count)) for t in tokens]
    place = []
    for i in range(count):
        rank = owner[i] * pair
        for j in range(i):
            rank = rank + jnp.where(owner[j] == owner[i], 1, 0)
        place.append(rank)
    order, local = [], []
    for d in range(count):
        at, slot = jnp.int32(0), jnp.int32(0)
        for i in range(count):
            hit = place[i] == d
            at = jnp.where(hit, i, at)
            slot = jnp.where(hit, tokens[i], slot)
        order.append(at)
        local.append(lax.rem(slot, jnp.int32(count)))
    return order, local


def layer_kernel(dims, names, *refs):
    (
        lengths, table, stream, att_routes, att_gate, mlp_routes, mlp_gate, gain_attn, gain_mlp, freq,
        w_query, w_key, w_value, w_out, w_gate, w_up, w_down, pages,
        hidden, arrived, slots,
    ) = refs[:21]
    b = types.SimpleNamespace(**dict(zip(names, refs[21:])))
    tp_count, grp_count, cap = dims
    tp = lax.axis_index("tp")
    grp = lax.axis_index("grp")
    core = grp % 2
    rows, model = stream.shape
    tok = rows * tp_count
    width = model // tp_count
    heads = width // HD
    hid = w_gate.shape[1]
    reach = grp_count // 2
    window = (reach + 1) * tok
    hops = reach // 2
    pages_dev = pages.shape[0]
    pair = pages_dev // grp_count
    rounds = pair * PIECES
    peers = tp_count - 1
    square = tp_count == 4
    nx = tp + 1 - 2 * (tp % 2)
    ny = (tp + 2) % 4
    nd = 3 - tp

    def remote(src, dst, send, recv, peer):
        return pltpu.make_async_remote_copy(src, dst, send, recv, peer, MESH)

    def lanes_of(owner):
        return pl.ds(pl.multiple_of(owner * width, 128), width)

    def gather(block, whole, send, recv):
        if square:
            own = [
                remote(block(tp, 0), block(tp, 0), send.at[0], recv.at[0], {"tp": nx}),
                remote(block(tp, 1), block(tp, 1), send.at[2], recv.at[2], {"tp": ny}),
                remote(block(tp, 1), block(tp, 1), send.at[1], recv.at[1], {"tp": nx}),
                remote(block(tp, 0), block(tp, 0), send.at[3], recv.at[3], {"tp": ny}),
            ]
            on = [
                remote(block(nx, 0), block(nx, 0), send.at[4], recv.at[4], {"tp": ny}),
                remote(block(ny, 1), block(ny, 1), send.at[5], recv.at[5], {"tp": nx}),
            ]
        else:
            own = [
                remote(
                    whole(tp), whole(tp), send.at[j - 1], recv.at[j - 1],
                    {"tp": (tp + j) % tp_count},
                )
                for j in range(1, tp_count)
            ]
            on = []

        def start():
            for copy in own:
                copy.start()

        def forward():
            for first, copy in zip(own, on):
                first.wait_recv()
                copy.start()

        late = [[copy] for copy in own[len(on):]] + ([on] if on else [])

        def arrive(k):
            for copy in late[k]:
                copy.wait_recv()

        def finish():
            for k in range(len(late)):
                arrive(k)

        def drain():
            for copy in own + on:
                copy.wait_send()

        return types.SimpleNamespace(
            own=own, start=start, forward=forward, arrive=arrive, finish=finish, drain=drain
        )

    def scatter(count, base, p_out, p_in, s_out, s_in, send, recv):
        half = count // 2
        upper, lower = pl.ds(base, half), pl.ds(base + half, half)
        if square:
            kx = [
                remote(p_out.at[i], p_in.at[i], send.at[i], recv.at[i], {"tp": nx})
                for i in range(2)
            ]
            ky = [
                remote(p_out.at[i], p_in.at[i], send.at[i], recv.at[i], {"tp": ny})
                for i in range(2, 4)
            ]
            k2 = remote(s_out.at[0], s_in.at[0], send.at[4], recv.at[4], {"tp": ny})
            k3 = remote(s_out.at[1], s_in.at[1], send.at[5], recv.at[5], {"tp": nx})
            copies = kx + ky + [k2, k3]
        else:
            copies = [
                remote(
                    p_out.at[j - 1], p_in.at[j - 1], send.at[j - 1], recv.at[j - 1],
                    {"tp": (tp + j) % tp_count},
                )
                for j in range(1, tp_count)
            ]

        def emit(part):
            if square:
                far = part(nd)
                p_out[1] = far[:half].astype(bf16)
                kx[1].start()
                p_out[3] = far[half:].astype(bf16)
                ky[1].start()
                side = part(nx)
                p_out[0] = side[:half].astype(bf16)
                kx[0].start()
                b.acc[lower, lanes_of(nx)] = side[half:]
                side = part(ny)
                p_out[2] = side[half:].astype(bf16)
                ky[0].start()
                b.acc[upper, lanes_of(ny)] = side[:half]
            else:
                for j in range(1, tp_count):
                    p_out[j - 1] = part((tp + j) % tp_count).astype(bf16)
                    copies[j - 1].start()
            b.acc[pl.ds(base, count), lanes_of(tp)] = part(tp)

        def middle():
            if square:
                kx[1].wait_recv()
                s_out[0] = (b.acc[upper, lanes_of(ny)] + p_in[1].astype(f32)).astype(bf16)
                k2.start()
                ky[1].wait_recv()
                s_out[1] = (b.acc[lower, lanes_of(nx)] + p_in[3].astype(f32)).astype(bf16)
                k3.start()

        def result():
            top, low = b.acc[upper, lanes_of(tp)], b.acc[lower, lanes_of(tp)]
            if square:
                for copy in (kx[0], ky[0], k2, k3):
                    copy.wait_recv()
                top = top + p_in[0].astype(f32) + s_in[0].astype(f32)
                low = low + p_in[2].astype(f32) + s_in[1].astype(f32)
            else:
                for j, copy in enumerate(copies):
                    copy.wait_recv()
                    top = top + p_in[j, 0:half].astype(f32)
                    low = low + p_in[j, half:count].astype(f32)
            return top, low

        def drain():
            for copy in copies:
                copy.wait_send()

        return types.SimpleNamespace(emit=emit, middle=middle, result=result, drain=drain)

    load_pages = pltpu.make_async_copy(pages, b.held, b.page_sem.at[0])
    load_pages.start()
    load_k = pltpu.make_async_copy(w_key, b.wkv.at[:, pl.ds(0, width)], b.kv_sem.at[0])
    load_v = pltpu.make_async_copy(w_value, b.wkv.at[:, pl.ds(width, width)], b.kv_sem.at[1])
    load_k.start()
    load_v.start()
    room = min(E_ATT, b.wide.shape[1] // width)
    load_q = [
        pltpu.make_async_copy(
            w_query.at[e], b.wide.at[:, pl.ds((e % room) * width, width)], b.q_sem.at[e]
        )
        for e in range(E_ATT)
    ]
    for load in load_q[:room]:
        load.start()
    load_o = [
        [
            pltpu.make_async_copy(
                w_out.at[e, pl.ds(h * HD, HD)], b.wo.at[h, pl.ds(e * HD, HD)], b.o_sem.at[h, e]
            )
            for e in range(E_ATT)
        ]
        for h in range(heads)
    ]

    @pl.when(grp < reach)
    def _():
        b.kv[:, :reach] = jnp.zeros((heads, reach, tok, 2 * HD), bf16)

    barrier = pltpu.get_barrier_semaphore()
    for j in range(1, tp_count):
        pl.semaphore_signal(
            barrier, inc=1, device_id={"tp": (tp + j) % tp_count}, device_id_type=MESH
        )
    for j in range(1, grp_count):
        pl.semaphore_signal(
            barrier, inc=1, device_id={"grp": (grp + j) % grp_count}, device_id_type=MESH
        )

    index = lax.broadcasted_iota(jnp.int32, (tok, 1), 0) + grp * tok
    starts = jnp.zeros((tok, 1), jnp.int32)
    end = jnp.int32(0)
    for r in range(lengths.shape[0]):
        end = end + lengths[r]
        starts = jnp.where(index >= end, end, starts)
    angles = (index - starts).astype(f32) * freq[...]
    b.cosine[...] = jnp.cos(angles)
    sign = jnp.where(lax.broadcasted_iota(jnp.int32, (1, HD), 1) < HD // 2, -1.0, 1.0)
    b.sine[...] = jnp.sin(angles) * sign
    column = lax.broadcasted_iota(jnp.int32, (tok, window), 1) + (grp - reach) * tok
    b.bias[...] = jnp.where((column <= index) & (column >= starts), 0.0, masked_score)

    mine = pl.ds(pl.multiple_of(tp * rows, rows), rows)
    b.rows_all[mine, :] = stream[...]
    fields = [
        ref[...].astype(f32) for ref in (att_routes, att_gate, mlp_routes, mlp_gate)
    ]
    fields = jnp.concatenate(fields + [jnp.zeros((META - 4 * TOPK, rows), f32)], axis=0)
    b.info[mine, :] = flip(fields, rows).astype(bf16)
    with scope("entry_wait"):
        pl.semaphore_wait(barrier, tp_count - 1 + grp_count - 1)

    def row_block(owner, half):
        size = rows // 2
        return b.rows_all.at[pl.ds(pl.multiple_of(owner * rows + half * size, 16), size)]

    def row_whole(owner):
        return b.rows_all.at[pl.ds(pl.multiple_of(owner * rows, rows), rows)]

    rows_gather = gather(row_block, row_whole, b.row_send, b.row_recv)
    rows_gather.start()
    info_copies = [
        remote(
            b.info.at[mine], b.info.at[mine], b.info_send.at[j - 1], b.info_recv.at[j - 1],
            {"tp": (tp + j) % tp_count},
        )
        for j in range(1, tp_count)
    ]
    for copy in info_copies:
        copy.start()

    page_copies = []

    def pick_pages(n, order):
        for p in range(grp_count):
            for half in range(PIECES):
                b.staged[n, half, p] = b.held[order[p * pair + n], half]

    turns = {False: [], True: []}

    def at_rounds(name):
        for up in (False, True):
            left = rounds - len(turns[up])
            count = left if name == "last" else min(left, WHEN[name][up] * rounds // 8)
            for _ in range(count):
                send_pages(len(turns[up]), up)
                turns[up].append(name)

    def send_pages(turn_index, up):
        n, part = turn_index // PIECES, turn_index % PIECES
        if not up:
            keep = pltpu.make_async_copy(
                b.staged.at[n, part, grp], arrived.at[grp, n, part], b.self_sem.at[turn_index]
            )
            keep.start()
            page_copies.append(keep)
        for j in range(1, grp_count):
            peer = (grp + j) % grp_count
            copy = remote(
                b.staged.at[n, part, peer], arrived.at[grp, n, part],
                b.page_send.at[turn_index, j - 1], b.page_recv.at[turn_index, j - 1],
                {"grp": peer},
            )
            pl.when(grp + j < grp_count if up else grp + j >= grp_count)(copy.start)
            if up:
                page_copies.append(copy)

    def begin_pages():
        order, local = page_scalars(table, pages_dev, pair)
        lane = lax.broadcasted_iota(jnp.int32, (1, META), 1)
        for p in range(grp_count):
            line = jnp.zeros((1, META), jnp.int32)
            for n in range(pair):
                line = jnp.where(lane == n, local[p * pair + n], line)
            b.slot_out[p] = line
        with scope("load_pages"):
            load_pages.wait()
        with scope("pick"):
            for n in range(pair):
                pick_pages(n, order)
        slots[grp] = b.slot_out[grp]
        for j in range(1, grp_count):
            peer = (grp + j) % grp_count
            copy = remote(
                b.slot_out.at[peer], slots.at[grp], b.slot_send.at[j - 1], b.slot_recv.at[j - 1],
                {"grp": peer},
            )
            copy.start()
            page_copies.append(copy)

    onward = {"grp": (grp + 2) % grp_count}
    other = {"grp": grp + 1 - 2 * core}
    rings = [
        [
            remote(
                b.kv.at[h, reach - 2 * n], b.kv.at[h, reach - 2 * n - 2],
                b.ring_send.at[h, n], b.ring_recv.at[h, n], onward,
            )
            for n in range(1, hops)
        ]
        for h in range(heads)
    ]
    sides = [
        [
            remote(
                b.kv.at[h, reach - 2 * (core + n)], b.kv.at[h, reach - 1 - 2 * n],
                b.side_send.at[h, n], b.side_recv.at[h, n], other,
            )
            for n in range(hops)
        ]
        for h in range(heads)
    ]
    if square:
        owners = [tp, nx, ny, nd]
    else:
        owners = [(tp + tp_count - j) % tp_count for j in range(tp_count)]
    first_hop = []
    for c, owner in enumerate(owners):
        if c:
            with scope(f"arrive{c}"):
                rows_gather.arrive(c - 1)
        span = pl.ds(pl.multiple_of(owner * rows, rows), rows)
        widened = b.rows_all[span, :].astype(f32)
        mean_square = jnp.mean(widened * widened, axis=-1, keepdims=True)
        chunk = (widened * lax.rsqrt(mean_square + epsilon) * gain_attn[...]).astype(bf16)
        b.normed[span, :] = chunk
        if c == 0:
            with scope("kv_load"):
                load_k.wait()
                load_v.wait()
        cosine, sine = b.cosine[span, :], b.sine[span, :]
        for two in range(heads // 2):
            at = two * 2 * HD
            keys = jnp.dot(chunk, b.wkv[:, at : at + 2 * HD], preferred_element_type=f32)
            values = jnp.dot(
                chunk, b.wkv[:, width + at : width + at + 2 * HD], preferred_element_type=f32
            )
            for i in range(2):
                part = slice(i * HD, (i + 1) * HD)
                h = 2 * two + i
                b.kv[h, reach, span, :HD] = turn(keys[:, part], cosine, sine).astype(bf16)
                b.kv[h, reach, span, HD:] = values[:, part].astype(bf16)
        copy = remote(
            b.kv.at[:, reach, span], b.kv.at[:, reach - 2, span],
            b.hop_send.at[c], b.hop_recv.at[c], onward,
        )
        pl.when(grp + 2 < grp_count)(copy.start)
        first_hop.append(copy)
        if c == 0:
            with scope("rows_forward"):
                rows_gather.forward()
            for load in [x for line in load_o for x in line]:
                load.start()
            begin_pages()
            at_rounds("early")
    b.mid[...] = b.rows_all[:, lanes_of(tp)]

    for copy in info_copies:
        copy.wait_recv()
    ids = b.info[...].astype(f32)

    def project(e):
        load_q[e].wait()
        at = (e % room) * width
        projected = jnp.dot(b.normed[...], b.wide[:, at : at + width], preferred_element_type=f32)
        if e + room < E_ATT:
            load_q[e + room].start()
        for k in range(TOPK):
            total = b.acc[:tok, k * width : (k + 1) * width] if e else 0.0
            b.acc[:tok, k * width : (k + 1) * width] = jnp.where(
                ids[:, k : k + 1] == float(e), projected, total
            )

    for e in range(E_ATT):
        with scope(f"project{e}"):
            project(e)
    with scope("hop0"):
        @pl.when(grp >= 2)
        def _():
            for copy in first_hop:
                copy.wait_recv()

    for n in range(hops - 1):
        for h in range(heads):
            if n:
                pl.when(grp >= 2)(rings[h][n - 1].wait_recv)
            pl.when(grp + 2 < grp_count)(rings[h][n].start)
            sides[h][n].start()
    wide_loads = [
        pltpu.make_async_copy(w_gate, b.wg, b.w_sem.at[0])
        if hasattr(b, "wg")
        else pltpu.make_async_copy(w_gate, b.wide.at[:, pl.ds(0, hid)], b.w_sem.at[0]),
        pltpu.make_async_copy(w_up, b.wu, b.w_sem.at[1])
        if hasattr(b, "wu")
        else pltpu.make_async_copy(w_up, b.wide.at[:, pl.ds(hid, hid)], b.w_sem.at[1]),
    ]
    for load in wide_loads:
        load.start()
    for k in range(TOPK):
        for h in range(heads):
            at = k * width + h * HD
            b.query[k, h] = turn(
                b.acc[:tok, at : at + HD], b.cosine[...], b.sine[...]
            ).astype(bf16)

    across = lax.dot_general(
        eye(META), ids.astype(bf16), (((1,), (1,)), ((), ())), preferred_element_type=f32
    )
    lower_mask = (
        lax.broadcasted_iota(jnp.int32, (tok, tok), 0)
        < lax.broadcasted_iota(jnp.int32, (tok, tok), 1)
    ).astype(bf16)
    at = 2 * TOPK
    hits, weigh = [], []
    for e in range(E_MLP):
        hot = [across[at + k : at + k + 1, :] == float(e) for k in range(TOPK)]
        gates = [
            jnp.where(hot[k], across[at + TOPK + k : at + TOPK + k + 1, :], 0.0)
            for k in range(TOPK)
        ]
        weigh.append(gates[0] + gates[1])
        hits.append(jnp.where(hot[0] | hot[1], 1.0, 0.0))
    hit = jnp.concatenate(hits, axis=0)
    rank = jnp.dot(hit.astype(bf16), lower_mask, preferred_element_type=f32)
    rank = jnp.where(hit > 0.5, rank, -1.0)
    slot_ids = lax.broadcasted_iota(jnp.int32, (cap, tok), 0).astype(f32)
    per_owner = grp_count // E_MLP
    for e in range(E_MLP):
        placed = rank[e : e + 1, :] == slot_ids
        b.select[e * cap : (e + 1) * cap, :] = jnp.where(placed, 1.0, 0.0).astype(bf16)
        value = jnp.where(placed, weigh[e], 0.0).astype(bf16)
        for i in range(per_owner):
            g = e * per_owner + i
            b.mix[g * cap : (g + 1) * cap, :] = value

    scale = HD ** (-0.5)
    down_rows = E_ATT * HD
    down_parts = [
        (c, min(down_rows, hid - c * down_rows)) for c in range(-(-hid // down_rows))
    ]
    down_loads = [
        pltpu.make_async_copy(
            w_down.at[pl.ds(c * down_rows, size)], b.wo.at[c, pl.ds(0, size)], b.w_sem.at[2 + c]
        )
        for c, size in down_parts
    ]

    def ready(h):
        with scope(f"ring_last{h}"):
            pl.when(grp >= 2)(rings[h][hops - 2].wait_recv)
        sides[h][hops - 1].start()

    ready(0)
    out_scatter = scatter(tok, 0, b.po2, b.pi2, b.so2, b.si2, b.s2_send, b.s2_recv)
    for h in range(heads):
        for n in range(hops):
            with scope(f"side_wait{h}"):
                sides[h][n].wait_recv()
        key_head = b.kv[h, :, :, :HD].reshape(window, HD)
        value_head = b.kv[h, :, :, HD:].reshape(window, HD)
        att = []
        for k in range(TOPK):
            scores = lax.dot_general(
                b.query[k, h], key_head, (((1,), (1,)), ((), ())), preferred_element_type=f32
            ) + b.bias[...]
            top = jnp.max(scores, axis=-1, keepdims=True)
            weights = jnp.exp((scores - top) * scale)
            weight_sum = jnp.sum(weights, axis=-1, keepdims=True)
            summed = jnp.dot(weights.astype(bf16), value_head, preferred_element_type=f32)
            att.append(summed / weight_sum)
        if h + 1 < heads:
            ready(h + 1)
        else:
            at_rounds("kv")
        for e in range(E_ATT):
            mixed = None
            for k in range(TOPK):
                gate = jnp.where(
                    ids[:, k : k + 1] == float(e), ids[:, TOPK + k : TOPK + k + 1], 0.0
                )
                term = gate * att[k]
                mixed = term if mixed is None else mixed + term
            b.normed[:, e * HD : (e + 1) * HD] = mixed.astype(bf16)
        with scope(f"wo_wait{h}"):
            for load in load_o[h]:
                load.wait()
        if h + 1 < heads:
            for j in range(tp_count):
                lanes = slice(j * width, (j + 1) * width)
                part = jnp.dot(
                    b.normed[:, :down_rows], b.wo[h, :, lanes], preferred_element_type=f32
                )
                b.acc[:tok, lanes] = part if h == 0 else b.acc[:tok, lanes] + part
            if h < len(down_loads):
                down_loads[h].start()
        else:

            def last_part(owner):
                return b.acc[:tok, lanes_of(owner)] + jnp.dot(
                    b.normed[:, :down_rows], b.wo[h, :, lanes_of(owner)],
                    preferred_element_type=f32,
                )

            with scope("emit2"):
                out_scatter.emit(last_part)
    with scope("middle2"):
        out_scatter.middle()
    with scope("result2"):
        top, low = out_scatter.result()
    half = tok // 2
    b.mid[:half, :] = (b.mid[:half, :].astype(f32) + top).astype(bf16)
    b.mid[half:, :] = (b.mid[half:, :].astype(f32) + low).astype(bf16)

    rows_gather.drain()

    step_rows = STEP_BLOCKS * cap
    steps = grp_count // STEP_BLOCKS
    def step_gather(step):
        def block(owner, half):
            return b.gathered.at[owner, pl.ds((STEP_BLOCKS * step + half) * cap, cap)]

        def whole(owner):
            return b.gathered.at[owner, pl.ds(step * step_rows, step_rows)]

        return gather(block, whole, b.g_send.at[step], b.g_recv.at[step])

    gathers = [step_gather(s) for s in range(steps)]
    own = pl.multiple_of(grp // per_owner * cap, cap)
    b.gathered[tp, 0:cap, :] = jnp.dot(
        b.select[pl.ds(own, cap), :], b.mid[...], preferred_element_type=f32
    ).astype(bf16)
    early = [gathers[0].own[0], gathers[0].own[3]] if square else []
    for copy in early:
        copy.start()
    for e in range(E_MLP):
        b.picked[e] = jnp.dot(
            b.select[e * cap : (e + 1) * cap, :], b.mid[...], preferred_element_type=f32
        ).astype(bf16)
    dispatch = []
    for i in range(1, grp_count):
        peer = (grp + grp_count - i) % grp_count
        copy = remote(
            b.picked.at[peer // per_owner], b.gathered.at[tp, pl.ds(i * cap, cap)],
            b.d_send.at[i - 1], b.d_recv.at[i - 1], {"grp": peer},
        )
        copy.start()
        dispatch.append(copy)
    scatters = [
        scatter(
            step_rows, (s % 2) * step_rows, b.po3.at[s], b.pi3.at[s], b.so3.at[s], b.si3.at[s],
            b.s3_send.at[s], b.s3_recv.at[s],
        )
        for s in range(steps)
    ]

    def pass_on(step):
        for i in range(step * STEP_BLOCKS, (step + 1) * STEP_BLOCKS):
            if i:
                dispatch[i - 1].wait_recv()
        for n, copy in enumerate(gathers[step].own):
            if step or not (square and n in (0, 3)):
                copy.start()

    ret = []

    def give_back(step):
        for q, value in enumerate(scatters[step].result()):
            i = step * STEP_BLOCKS + q
            back = pl.ds(pl.multiple_of(grp * cap, cap), cap)
            if i == 0:
                b.ret_in[back, :] = value.astype(bf16)
            else:
                b.ret_out[i * cap : (i + 1) * cap, :] = value.astype(bf16)
                copy = remote(
                    b.ret_out.at[pl.ds(i * cap, cap)], b.ret_in.at[back],
                    b.t_send.at[i - 1], b.t_recv.at[i - 1], {"grp": (grp + i) % grp_count},
                )
                copy.start()
                ret.append(copy)

    with scope("pass0"):
        pass_on(0)
    with scope("forward0"):
        gathers[0].forward()
    with scope("pass1"):
        pass_on(1)
    at_rounds("out")
    if steps > 2:
        with scope("pass2"):
            pass_on(2)
    for load in wide_loads + down_loads:
        load.wait()
    for step in range(steps):
        part = slice(step * step_rows, (step + 1) * step_rows)
        with scope(f"finish{step}"):
            gathers[step].finish()
        if step == 0 and steps > 1:
            with scope("forward1"):
                gathers[1].forward()
        square_sum = None
        for s in range(tp_count):
            block = b.gathered[s, part, :].astype(f32)
            term = jnp.sum(block * block, axis=-1, keepdims=True)
            square_sum = term if square_sum is None else square_sum + term
        factor = lax.rsqrt(square_sum * (1.0 / model) + epsilon)
        for s in range(tp_count):
            lanes = slice(s * width, (s + 1) * width)
            b.rows_all[:step_rows, lanes] = (
                b.gathered[s, part, :].astype(f32) * factor * gain_mlp[:, lanes]
            ).astype(bf16)
        xn = b.rows_all[:step_rows, :]
        wg = b.wg[...] if hasattr(b, "wg") else b.wide[:, :hid]
        wu = b.wu[...] if hasattr(b, "wu") else b.wide[:, hid : 2 * hid]
        gate = jnp.dot(xn, wg, preferred_element_type=f32)
        up = jnp.dot(xn, wu, preferred_element_type=f32)
        units = (gate / (1.0 + jnp.exp(-gate)) * up).astype(bf16)
        if step + 3 < steps:
            with scope(f"pass{step+3}"):
                pass_on(step + 3)
        if step + 2 < steps:
            with scope(f"forward{step+2}"):
                gathers[step + 2].forward()
        if step == 0:
            at_rounds("disp")
        elif step == 1:
            at_rounds("last")
        if step >= 1:
            with scope(f"mid{step-1}"):
                scatters[step - 1].middle()
        if step >= 2:
            with scope(f"give{step-2}"):
                give_back(step - 2)

        def down(owner):
            total = None
            for c, size in down_parts:
                term = jnp.dot(
                    units[:, c * down_rows : c * down_rows + size],
                    b.wo[c, :size, lanes_of(owner)], preferred_element_type=f32,
                )
                total = term if total is None else total + term
            return total

        with scope(f"emit3_{step}"):
            scatters[step].emit(down)
    if steps >= 2:
        with scope(f"give{steps-2}"):
            give_back(steps - 2)
    with scope(f"mid{steps-1}"):
        scatters[steps - 1].middle()
    with scope(f"give{steps-1}"):
        give_back(steps - 1)
    with scope("ret_wait"):
        for copy in ret:
            copy.wait_recv()
    hidden[...] = (
        b.mid[...].astype(f32)
        + lax.dot_general(
            b.mix[...], b.ret_in[...], (((0,), (0,)), ((), ())), preferred_element_type=f32
        )
    ).astype(bf16)
    with scope("page_wait"):
        for copy in page_copies:
            copy.wait()
    for copy in info_copies + dispatch + ret + [x for line in sides for x in line]:
        copy.wait_send()

    @pl.when(grp + 2 < grp_count)
    def _():
        for copy in first_hop + [x for line in rings for x in line]:
            copy.wait_send()

    for group in [out_scatter] + gathers + scatters:
        group.drain()


def place_kernel(slot_of, arrived, layer_out, placed, hidden_out, held, rows, isem, osem):
    groups, pair = arrived.shape[:2]
    reads = [
        pltpu.make_async_copy(
            arrived.at[i // pair, i % pair], held.at[i], isem.at[i]
        )
        for i in range(groups * pair)
    ]
    writes = [
        pltpu.make_async_copy(
            held.at[i], placed.at[slot_of[i // pair, 0, i % pair]], osem.at[i]
        )
        for i in range(groups * pair)
    ]
    reads.append(pltpu.make_async_copy(layer_out, rows, isem.at[groups * pair]))
    writes.append(pltpu.make_async_copy(rows, hidden_out, osem.at[groups * pair]))
    for copy in reads:
        copy.start()
    for read, write in zip(reads, writes):
        read.wait()
        write.start()
    for copy in writes:
        copy.wait()


def on_device(
    stream,
    lengths,
    att_routes,
    att_gate,
    mlp_routes,
    mlp_gate,
    gain_attn,
    gain_mlp,
    w_query,
    w_key,
    w_value,
    w_output,
    w_gate,
    w_up,
    w_down,
    cache_in,
    page_table,
):
    grp_count = lax.axis_size("grp")
    tp_count = lax.axis_size("tp")
    rows, model = stream.shape
    tok = rows * tp_count
    width = w_key.shape[1]
    heads = width // HD
    hid = w_gate.shape[1]
    pages_dev = page_table.shape[0]
    pair = pages_dev // grp_count
    dma = pltpu.SemaphoreType.DMA
    sds = jax.ShapeDtypeStruct
    vmem = pltpu.VMEM
    peers = tp_count - 1
    square = tp_count == 4
    cap = tok * TOPK * 5 // (E_MLP * 4)
    reach = grp_count // 2
    hops = reach // 2
    window = (reach + 1) * tok
    step_rows = STEP_BLOCKS * cap
    steps = grp_count // STEP_BLOCKS
    slots = grp_count * cap
    rounds = pair * PIECES

    frequency = rope_base ** (-(np.arange(HD // 2) * 2.0 / HD))
    freq = jnp.asarray(np.concatenate([frequency, frequency])[None, :], f32)
    page_len = tok // pages_dev
    piece = (page_len // PIECES * cache_in.shape[1] * cache_in.shape[2],) + cache_in.shape[3:]
    pages = cache_in.reshape((pages_dev, PIECES) + piece)

    scratch = {
        "held": vmem((pages_dev, PIECES) + piece, bf16),
        "staged": vmem((pair, PIECES, grp_count) + piece, bf16),
        "slot_out": vmem((grp_count, 1, META), jnp.int32),
        "wkv": vmem((model, 2 * width), bf16),
        "wo": vmem((heads, E_ATT * HD, model), bf16),
        "rows_all": vmem((max(tok, step_rows), model), bf16),
        "normed": vmem((tok, model), bf16),
        "info": vmem((tok, META), bf16),
        "cosine": vmem((tok, HD), f32),
        "sine": vmem((tok, HD), f32),
        "bias": vmem((tok, window), f32),
        "kv": vmem((heads, reach + 1, tok, 2 * HD), bf16),
        "query": vmem((TOPK, heads, tok, HD), bf16),
        "acc": vmem((max(tok, 2 * step_rows), model), f32),
        "mid": vmem((tok, width), bf16),
        "select": vmem((E_MLP * cap, tok), bf16),
        "mix": vmem((slots, tok), bf16),
        "picked": vmem((E_MLP, cap, width), bf16),
        "gathered": vmem((tp_count, slots, width), bf16),
        "ret_out": vmem((slots, width), bf16),
        "ret_in": vmem((slots, width), bf16),
        "page_sem": dma((1,)),
        "kv_sem": dma((2,)),
        "q_sem": dma((E_ATT,)),
        "o_sem": dma((heads, E_ATT)),
        "w_sem": dma((2 + heads,)),
        "row_send": dma((max(6, peers),)),
        "row_recv": dma((max(6, peers),)),
        "info_send": dma((peers,)),
        "info_recv": dma((peers,)),
        "self_sem": dma((rounds,)),
        "page_send": dma((rounds, grp_count - 1)),
        "page_recv": dma((rounds, grp_count - 1)),
        "slot_send": dma((grp_count - 1,)),
        "slot_recv": dma((grp_count - 1,)),
        "hop_send": dma((tp_count,)),
        "hop_recv": dma((tp_count,)),
        "ring_send": dma((heads, hops)),
        "ring_recv": dma((heads, hops)),
        "side_send": dma((heads, hops)),
        "side_recv": dma((heads, hops)),
        "s2_send": dma((max(6, peers),)),
        "s2_recv": dma((max(6, peers),)),
        "d_send": dma((grp_count - 1,)),
        "d_recv": dma((grp_count - 1,)),
        "g_send": dma((steps, max(6, peers))),
        "g_recv": dma((steps, max(6, peers))),
        "s3_send": dma((steps, max(6, peers))),
        "s3_recv": dma((steps, max(6, peers))),
        "t_send": dma((grp_count - 1,)),
        "t_recv": dma((grp_count - 1,)),
    }
    if hid % 128 == 0:
        scratch["wide"] = vmem((model, 2 * hid), bf16)
    else:
        scratch["wide"] = vmem((model, E_ATT * width), bf16)
        scratch["wg"] = vmem((model, hid), bf16)
        scratch["wu"] = vmem((model, hid), bf16)
    for stage, lead, count in (("2", (), tok), ("3", (steps,), step_rows)):
        if square:
            part, second = lead + (4, count // 2, width), lead + (2, count // 2, width)
        else:
            part, second = lead + (peers, count, width), lead + (1, 16, 128)
        scratch["po" + stage] = vmem(part, bf16)
        scratch["pi" + stage] = vmem(part, bf16)
        scratch["so" + stage] = vmem(second, bf16)
        scratch["si" + stage] = vmem(second, bf16)

    layer_out, arrived, slot_of = pl.pallas_call(
        functools.partial(layer_kernel, (tp_count, grp_count, cap), tuple(scratch)),
        out_shape=(
            sds((tok, width), bf16),
            sds((grp_count, pair, PIECES) + piece, bf16),
            sds((grp_count, 1, META), jnp.int32),
        ),
        in_specs=[SM] * 2 + [VM] * 8 + [ANY] * 8,
        out_specs=(VM, ANY, VM),
        scratch_shapes=list(scratch.values()),
        compiler_params=pltpu.CompilerParams(
            vmem_limit_bytes=VMEM_LIMIT, collective_id=1, has_side_effects=True
        ),
        name="layer",
    )(
        lengths, page_table, stream, att_routes.T, att_gate.T, mlp_routes.T, mlp_gate.T,
        gain_attn[None, :], gain_mlp[None, :], freq,
        w_query, w_key, w_value, w_output, w_gate, w_up, w_down, pages,
    )

    cache_out, hidden_out = pl.pallas_call(
        place_kernel,
        out_shape=(sds((pages_dev, PIECES) + piece, bf16), sds((tok, width), bf16)),
        in_specs=[SM, ANY, ANY],
        out_specs=(ANY, ANY),
        scratch_shapes=[
            vmem((pages_dev, PIECES) + piece, bf16),
            vmem((tok, width), bf16),
            dma((pages_dev + 1,)),
            dma((pages_dev + 1,)),
        ],
        compiler_params=pltpu.CompilerParams(vmem_limit_bytes=VMEM_LIMIT),
        name="place_pages",
    )(slot_of, arrived, layer_out)
    return (hidden_out, cache_out.reshape((pages_dev, page_len) + cache_in.shape[1:]))


def solution(mesh):
    return jax.shard_map(
        on_device,
        mesh=mesh,
        in_specs=(
            P(("grp", "tp"), None),
            P(),
            P(("grp", "tp"), None),
            P(("grp", "tp"), None),
            P(("grp", "tp"), None),
            P(("grp", "tp"), None),
            P(),
            P(),
            P(None, None, "tp"),
            P(None, "tp"),
            P(None, "tp"),
            P(None, "tp", None),
            P(None, ("grp", "tp")),
            P(None, ("grp", "tp")),
            P(("grp", "tp"), None),
            P("grp", None, None, "tp", None),
            P("grp"),
        ),
        out_specs=(P("grp", "tp"), P("grp", None, None, None, "tp", None)),
        check_vma=False,
    )
```

```python
import contextlib
import functools
import types

import jax
import jax.numpy as jnp
import numpy as np
from jax import lax
from jax.experimental import pallas as pl
from jax.experimental.pallas import tpu as pltpu
from jax.sharding import PartitionSpec as P

HD = 128
E_ATT = 8
E_MLP = 8
TOPK = 2
META = 128
STEP_BLOCKS = 2
PIECES = 4
WHEN = {"early": (3, 0), "kv": (2, 3), "out": (0, 0), "disp": (3, 5)}
MESH = pl.DeviceIdType.MESH
VMEM_LIMIT = 62 * 1024 * 1024
TRACE = False


epsilon = 1e-06
rope_base = 10000.0
masked_score = -1e30

ANY = pl.BlockSpec(memory_space=pl.ANY)
VM = pl.BlockSpec(memory_space=pltpu.VMEM)
SM = pl.BlockSpec(memory_space=pltpu.SMEM)

bf16 = jnp.bfloat16
f32 = jnp.float32


def scope(name):
    return jax.named_scope(name) if TRACE else contextlib.nullcontext()


def turn(part, cosine, sine):
    return part * cosine + pltpu.roll(part, HD // 2, 1) * sine


def eye(n):
    a = lax.broadcasted_iota(jnp.int32, (n, n), 0)
    return (a == lax.broadcasted_iota(jnp.int32, (n, n), 1)).astype(bf16)


def flip(values, size):
    return lax.dot_general(
        eye(size), values.astype(bf16), (((1,), (1,)), ((), ())), preferred_element_type=f32
    )


def page_scalars(table, count, pair):
    tokens = [table[i] for i in range(count)]
    owner = [lax.div(t, jnp.int32(count)) for t in tokens]
    place = []
    for i in range(count):
        rank = owner[i] * pair
        for j in range(i):
            rank = rank + jnp.where(owner[j] == owner[i], 1, 0)
        place.append(rank)
    order, local = [], []
    for d in range(count):
        at, slot = jnp.int32(0), jnp.int32(0)
        for i in range(count):
            hit = place[i] == d
            at = jnp.where(hit, i, at)
            slot = jnp.where(hit, tokens[i], slot)
        order.append(at)
        local.append(lax.rem(slot, jnp.int32(count)))
    return order, local


def layer_kernel(dims, names, *refs):
    (
        lengths, table, stream, att_routes, att_gate, mlp_routes, mlp_gate, gain_attn, gain_mlp, freq,
        w_query, w_key, w_value, w_out, w_gate, w_up, w_down, pages,
        hidden, arrived, slots,
    ) = refs[:21]
    b = types.SimpleNamespace(**dict(zip(names, refs[21:])))
    tp_count, grp_count, cap = dims
    tp = lax.axis_index("tp")
    grp = lax.axis_index("grp")
    core = grp % 2
    rows, model = stream.shape
    tok = rows * tp_count
    width = model // tp_count
    heads = width // HD
    hid = w_gate.shape[1]
    reach = grp_count // 2
    window = (reach + 1) * tok
    hops = reach // 2
    pages_dev = pages.shape[0]
    pair = pages_dev // grp_count
    rounds = pair * PIECES
    peers = tp_count - 1
    square = tp_count == 4
    nx = tp + 1 - 2 * (tp % 2)
    ny = (tp + 2) % 4
    nd = 3 - tp

    def remote(src, dst, send, recv, peer):
        return pltpu.make_async_remote_copy(src, dst, send, recv, peer, MESH)

    def lanes_of(owner):
        return pl.ds(pl.multiple_of(owner * width, 128), width)

    def gather(block, whole, send, recv):
        if square:
            own = [
                remote(block(tp, 0), block(tp, 0), send.at[0], recv.at[0], {"tp": nx}),
                remote(block(tp, 1), block(tp, 1), send.at[2], recv.at[2], {"tp": ny}),
                remote(block(tp, 1), block(tp, 1), send.at[1], recv.at[1], {"tp": nx}),
                remote(block(tp, 0), block(tp, 0), send.at[3], recv.at[3], {"tp": ny}),
            ]
            on = [
                remote(block(nx, 0), block(nx, 0), send.at[4], recv.at[4], {"tp": ny}),
                remote(block(ny, 1), block(ny, 1), send.at[5], recv.at[5], {"tp": nx}),
            ]
        else:
            own = [
                remote(
                    whole(tp), whole(tp), send.at[j - 1], recv.at[j - 1],
                    {"tp": (tp + j) % tp_count},
                )
                for j in range(1, tp_count)
            ]
            on = []

        def start():
            for copy in own:
                copy.start()

        def forward():
            for first, copy in zip(own, on):
                first.wait_recv()
                copy.start()

        late = [[copy] for copy in own[len(on):]] + ([on] if on else [])

        def arrive(k):
            for copy in late[k]:
                copy.wait_recv()

        def finish():
            for k in range(len(late)):
                arrive(k)

        def drain():
            for copy in own + on:
                copy.wait_send()

        return types.SimpleNamespace(
            own=own, start=start, forward=forward, arrive=arrive, finish=finish, drain=drain
        )

    def scatter(count, base, p_out, p_in, s_out, s_in, send, recv):
        half = count // 2
        upper, lower = pl.ds(base, half), pl.ds(base + half, half)
        if square:
            kx = [
                remote(p_out.at[i], p_in.at[i], send.at[i], recv.at[i], {"tp": nx})
                for i in range(2)
            ]
            ky = [
                remote(p_out.at[i], p_in.at[i], send.at[i], recv.at[i], {"tp": ny})
                for i in range(2, 4)
            ]
            k2 = remote(s_out.at[0], s_in.at[0], send.at[4], recv.at[4], {"tp": ny})
            k3 = remote(s_out.at[1], s_in.at[1], send.at[5], recv.at[5], {"tp": nx})
            copies = kx + ky + [k2, k3]
        else:
            copies = [
                remote(
                    p_out.at[j - 1], p_in.at[j - 1], send.at[j - 1], recv.at[j - 1],
                    {"tp": (tp + j) % tp_count},
                )
                for j in range(1, tp_count)
            ]

        def emit(part):
            if square:
                far = part(nd)
                p_out[1] = far[:half].astype(bf16)
                kx[1].start()
                p_out[3] = far[half:].astype(bf16)
                ky[1].start()
                side = part(nx)
                p_out[0] = side[:half].astype(bf16)
                kx[0].start()
                b.acc[lower, lanes_of(nx)] = side[half:]
                side = part(ny)
                p_out[2] = side[half:].astype(bf16)
                ky[0].start()
                b.acc[upper, lanes_of(ny)] = side[:half]
            else:
                for j in range(1, tp_count):
                    p_out[j - 1] = part((tp + j) % tp_count).astype(bf16)
                    copies[j - 1].start()
            b.acc[pl.ds(base, count), lanes_of(tp)] = part(tp)

        def middle():
            if square:
                kx[1].wait_recv()
                s_out[0] = (b.acc[upper, lanes_of(ny)] + p_in[1].astype(f32)).astype(bf16)
                k2.start()
                ky[1].wait_recv()
                s_out[1] = (b.acc[lower, lanes_of(nx)] + p_in[3].astype(f32)).astype(bf16)
                k3.start()

        def result():
            top, low = b.acc[upper, lanes_of(tp)], b.acc[lower, lanes_of(tp)]
            if square:
                for copy in (kx[0], ky[0], k2, k3):
                    copy.wait_recv()
                top = top + p_in[0].astype(f32) + s_in[0].astype(f32)
                low = low + p_in[2].astype(f32) + s_in[1].astype(f32)
            else:
                for j, copy in enumerate(copies):
                    copy.wait_recv()
                    top = top + p_in[j, 0:half].astype(f32)
                    low = low + p_in[j, half:count].astype(f32)
            return top, low

        def drain():
            for copy in copies:
                copy.wait_send()

        return types.SimpleNamespace(emit=emit, middle=middle, result=result, drain=drain)

    load_pages = pltpu.make_async_copy(pages, b.held, b.page_sem.at[0])
    load_pages.start()
    load_k = pltpu.make_async_copy(w_key, b.wkv.at[:, pl.ds(0, width)], b.kv_sem.at[0])
    load_v = pltpu.make_async_copy(w_value, b.wkv.at[:, pl.ds(width, width)], b.kv_sem.at[1])
    load_k.start()
    load_v.start()
    room = min(E_ATT, b.wide.shape[1] // width)
    load_q = [
        pltpu.make_async_copy(
            w_query.at[e], b.wide.at[:, pl.ds((e % room) * width, width)], b.q_sem.at[e]
        )
        for e in range(E_ATT)
    ]
    for load in load_q[:room]:
        load.start()
    load_o = [
        [
            pltpu.make_async_copy(
                w_out.at[e, pl.ds(h * HD, HD)], b.wo.at[h, pl.ds(e * HD, HD)], b.o_sem.at[h, e]
            )
            for e in range(E_ATT)
        ]
        for h in range(heads)
    ]

    @pl.when(grp < reach)
    def _():
        b.kv[:, :reach] = jnp.zeros((heads, reach, tok, 2 * HD), bf16)

    barrier = pltpu.get_barrier_semaphore()
    for j in range(1, tp_count):
        pl.semaphore_signal(
            barrier, inc=1, device_id={"tp": (tp + j) % tp_count}, device_id_type=MESH
        )
    for j in range(1, grp_count):
        pl.semaphore_signal(
            barrier, inc=1, device_id={"grp": (grp + j) % grp_count}, device_id_type=MESH
        )

    index = lax.broadcasted_iota(jnp.int32, (tok, 1), 0) + grp * tok
    starts = jnp.zeros((tok, 1), jnp.int32)
    end = jnp.int32(0)
    for r in range(lengths.shape[0]):
        end = end + lengths[r]
        starts = jnp.where(index >= end, end, starts)
    angles = (index - starts).astype(f32) * freq[...]
    b.cosine[...] = jnp.cos(angles)
    sign = jnp.where(lax.broadcasted_iota(jnp.int32, (1, HD), 1) < HD // 2, -1.0, 1.0)
    b.sine[...] = jnp.sin(angles) * sign
    column = lax.broadcasted_iota(jnp.int32, (tok, window), 1) + (grp - reach) * tok
    b.bias[...] = jnp.where((column <= index) & (column >= starts), 0.0, masked_score)

    mine = pl.ds(pl.multiple_of(tp * rows, rows), rows)
    b.rows_all[mine, :] = stream[...]
    fields = [
        ref[...].astype(f32) for ref in (att_routes, att_gate, mlp_routes, mlp_gate)
    ]
    fields = jnp.concatenate(fields + [jnp.zeros((META - 4 * TOPK, rows), f32)], axis=0)
    b.info[mine, :] = flip(fields, rows).astype(bf16)
    with scope("entry_wait"):
        pl.semaphore_wait(barrier, tp_count - 1 + grp_count - 1)

    def row_block(owner, half):
        size = rows // 2
        return b.rows_all.at[pl.ds(pl.multiple_of(owner * rows + half * size, 16), size)]

    def row_whole(owner):
        return b.rows_all.at[pl.ds(pl.multiple_of(owner * rows, rows), rows)]

    rows_gather = gather(row_block, row_whole, b.row_send, b.row_recv)
    rows_gather.start()
    info_copies = [
        remote(
            b.info.at[mine], b.info.at[mine], b.info_send.at[j - 1], b.info_recv.at[j - 1],
            {"tp": (tp + j) % tp_count},
        )
        for j in range(1, tp_count)
    ]
    for copy in info_copies:
        copy.start()

    page_copies = []

    def pick_pages(n, order):
        for p in range(grp_count):
            for half in range(PIECES):
                b.staged[n, half, p] = b.held[order[p * pair + n], half]

    turns = {False: [], True: []}

    def at_rounds(name):
        for up in (False, True):
            left = rounds - len(turns[up])
            count = left if name == "last" else min(left, WHEN[name][up] * rounds // 8)
            for _ in range(count):
                send_pages(len(turns[up]), up)
                turns[up].append(name)

    def send_pages(turn_index, up):
        n, part = turn_index // PIECES, turn_index % PIECES
        if not up:
            keep = pltpu.make_async_copy(
                b.staged.at[n, part, grp], arrived.at[grp, n, part], b.self_sem.at[turn_index]
            )
            keep.start()
            page_copies.append(keep)
        for j in range(1, grp_count):
            peer = (grp + j) % grp_count
            copy = remote(
                b.staged.at[n, part, peer], arrived.at[grp, n, part],
                b.page_send.at[turn_index, j - 1], b.page_recv.at[turn_index, j - 1],
                {"grp": peer},
            )
            pl.when(grp + j < grp_count if up else grp + j >= grp_count)(copy.start)
            if up:
                page_copies.append(copy)

    def begin_pages():
        order, local = page_scalars(table, pages_dev, pair)
        lane = lax.broadcasted_iota(jnp.int32, (1, META), 1)
        for p in range(grp_count):
            line = jnp.zeros((1, META), jnp.int32)
            for n in range(pair):
                line = jnp.where(lane == n, local[p * pair + n], line)
            b.slot_out[p] = line
        with scope("load_pages"):
            load_pages.wait()
        with scope("pick"):
            for n in range(pair):
                pick_pages(n, order)
        slots[grp] = b.slot_out[grp]
        for j in range(1, grp_count):
            peer = (grp + j) % grp_count
            copy = remote(
                b.slot_out.at[peer], slots.at[grp], b.slot_send.at[j - 1], b.slot_recv.at[j - 1],
                {"grp": peer},
            )
            copy.start()
            page_copies.append(copy)

    onward = {"grp": (grp + 2) % grp_count}
    other = {"grp": grp + 1 - 2 * core}
    rings = [
        [
            remote(
                b.kv.at[h, reach - 2 * n], b.kv.at[h, reach - 2 * n - 2],
                b.ring_send.at[h, n], b.ring_recv.at[h, n], onward,
            )
            for n in range(1, hops)
        ]
        for h in range(heads)
    ]
    sides = [
        [
            remote(
                b.kv.at[h, reach - 2 * (core + n)], b.kv.at[h, reach - 1 - 2 * n],
                b.side_send.at[h, n], b.side_recv.at[h, n], other,
            )
            for n in range(hops)
        ]
        for h in range(heads)
    ]
    if square:
        owners = [tp, nx, ny, nd]
    else:
        owners = [(tp + tp_count - j) % tp_count for j in range(tp_count)]
    first_hop = []
    for c, owner in enumerate(owners):
        if c:
            with scope(f"arrive{c}"):
                rows_gather.arrive(c - 1)
        span = pl.ds(pl.multiple_of(owner * rows, rows), rows)
        widened = b.rows_all[span, :].astype(f32)
        mean_square = jnp.mean(widened * widened, axis=-1, keepdims=True)
        chunk = (widened * lax.rsqrt(mean_square + epsilon) * gain_attn[...]).astype(bf16)
        b.normed[span, :] = chunk
        if c == 0:
            with scope("kv_load"):
                load_k.wait()
                load_v.wait()
        cosine, sine = b.cosine[span, :], b.sine[span, :]
        for two in range(heads // 2):
            at = two * 2 * HD
            keys = jnp.dot(chunk, b.wkv[:, at : at + 2 * HD], preferred_element_type=f32)
            values = jnp.dot(
                chunk, b.wkv[:, width + at : width + at + 2 * HD], preferred_element_type=f32
            )
            for i in range(2):
                part = slice(i * HD, (i + 1) * HD)
                h = 2 * two + i
                b.kv[h, reach, span, :HD] = turn(keys[:, part], cosine, sine).astype(bf16)
                b.kv[h, reach, span, HD:] = values[:, part].astype(bf16)
        copy = remote(
            b.kv.at[:, reach, span], b.kv.at[:, reach - 2, span],
            b.hop_send.at[c], b.hop_recv.at[c], onward,
        )
        pl.when(grp + 2 < grp_count)(copy.start)
        first_hop.append(copy)
        if c == 0:
            with scope("rows_forward"):
                rows_gather.forward()
            for load in [x for line in load_o for x in line]:
                load.start()
            begin_pages()
            at_rounds("early")
    b.mid[...] = b.rows_all[:, lanes_of(tp)]

    for copy in info_copies:
        copy.wait_recv()
    ids = b.info[...].astype(f32)

    def project(e):
        load_q[e].wait()
        at = (e % room) * width
        projected = jnp.dot(b.normed[...], b.wide[:, at : at + width], preferred_element_type=f32)
        if e + room < E_ATT:
            load_q[e + room].start()
        for k in range(TOPK):
            total = b.acc[:tok, k * width : (k + 1) * width] if e else 0.0
            b.acc[:tok, k * width : (k + 1) * width] = jnp.where(
                ids[:, k : k + 1] == float(e), projected, total
            )

    for e in range(E_ATT):
        with scope(f"project{e}"):
            project(e)
    with scope("hop0"):
        @pl.when(grp >= 2)
        def _():
            for copy in first_hop:
                copy.wait_recv()

    for n in range(hops - 1):
        for h in range(heads):
            if n:
                pl.when(grp >= 2)(rings[h][n - 1].wait_recv)
            pl.when(grp + 2 < grp_count)(rings[h][n].start)
            sides[h][n].start()
    wide_loads = [
        pltpu.make_async_copy(w_gate, b.wg, b.w_sem.at[0])
        if hasattr(b, "wg")
        else pltpu.make_async_copy(w_gate, b.wide.at[:, pl.ds(0, hid)], b.w_sem.at[0]),
        pltpu.make_async_copy(w_up, b.wu, b.w_sem.at[1])
        if hasattr(b, "wu")
        else pltpu.make_async_copy(w_up, b.wide.at[:, pl.ds(hid, hid)], b.w_sem.at[1]),
    ]
    for load in wide_loads:
        load.start()
    for k in range(TOPK):
        for h in range(heads):
            at = k * width + h * HD
            b.query[k, h] = turn(
                b.acc[:tok, at : at + HD], b.cosine[...], b.sine[...]
            ).astype(bf16)

    across = lax.dot_general(
        eye(META), ids.astype(bf16), (((1,), (1,)), ((), ())), preferred_element_type=f32
    )
    lower_mask = (
        lax.broadcasted_iota(jnp.int32, (tok, tok), 0)
        < lax.broadcasted_iota(jnp.int32, (tok, tok), 1)
    ).astype(bf16)
    at = 2 * TOPK
    hits, weigh = [], []
    for e in range(E_MLP):
        hot = [across[at + k : at + k + 1, :] == float(e) for k in range(TOPK)]
        gates = [
            jnp.where(hot[k], across[at + TOPK + k : at + TOPK + k + 1, :], 0.0)
            for k in range(TOPK)
        ]
        weigh.append(gates[0] + gates[1])
        hits.append(jnp.where(hot[0] | hot[1], 1.0, 0.0))
    hit = jnp.concatenate(hits, axis=0)
    rank = jnp.dot(hit.astype(bf16), lower_mask, preferred_element_type=f32)
    rank = jnp.where(hit > 0.5, rank, -1.0)
    slot_ids = lax.broadcasted_iota(jnp.int32, (cap, tok), 0).astype(f32)
    per_owner = grp_count // E_MLP
    for e in range(E_MLP):
        placed = rank[e : e + 1, :] == slot_ids
        b.select[e * cap : (e + 1) * cap, :] = jnp.where(placed, 1.0, 0.0).astype(bf16)
        value = jnp.where(placed, weigh[e], 0.0).astype(bf16)
        for i in range(per_owner):
            g = e * per_owner + i
            b.mix[g * cap : (g + 1) * cap, :] = value

    scale = HD ** (-0.5)
    down_rows = E_ATT * HD
    down_parts = [
        (c, min(down_rows, hid - c * down_rows)) for c in range(-(-hid // down_rows))
    ]
    down_loads = [
        pltpu.make_async_copy(
            w_down.at[pl.ds(c * down_rows, size)], b.wo.at[c, pl.ds(0, size)], b.w_sem.at[2 + c]
        )
        for c, size in down_parts
    ]

    def ready(h):
        with scope(f"ring_last{h}"):
            pl.when(grp >= 2)(rings[h][hops - 2].wait_recv)
        sides[h][hops - 1].start()

    ready(0)
    out_scatter = scatter(tok, 0, b.po2, b.pi2, b.so2, b.si2, b.s2_send, b.s2_recv)
    for h in range(heads):
        for n in range(hops):
            with scope(f"side_wait{h}"):
                sides[h][n].wait_recv()
        key_head = b.kv[h, :, :, :HD].reshape(window, HD)
        value_head = b.kv[h, :, :, HD:].reshape(window, HD)
        att = []
        for k in range(TOPK):
            scores = lax.dot_general(
                b.query[k, h], key_head, (((1,), (1,)), ((), ())), preferred_element_type=f32
            ) + b.bias[...]
            top = jnp.max(scores, axis=-1, keepdims=True)
            weights = jnp.exp((scores - top) * scale)
            weight_sum = jnp.sum(weights, axis=-1, keepdims=True)
            summed = jnp.dot(weights.astype(bf16), value_head, preferred_element_type=f32)
            att.append(summed / weight_sum)
        if h + 1 < heads:
            ready(h + 1)
        else:
            at_rounds("kv")
        for e in range(E_ATT):
            mixed = None
            for k in range(TOPK):
                gate = jnp.where(
                    ids[:, k : k + 1] == float(e), ids[:, TOPK + k : TOPK + k + 1], 0.0
                )
                term = gate * att[k]
                mixed = term if mixed is None else mixed + term
            b.normed[:, e * HD : (e + 1) * HD] = mixed.astype(bf16)
        with scope(f"wo_wait{h}"):
            for load in load_o[h]:
                load.wait()
        if h + 1 < heads:
            for j in range(tp_count):
                lanes = slice(j * width, (j + 1) * width)
                part = jnp.dot(
                    b.normed[:, :down_rows], b.wo[h, :, lanes], preferred_element_type=f32
                )
                b.acc[:tok, lanes] = part if h == 0 else b.acc[:tok, lanes] + part
            if h < len(down_loads):
                down_loads[h].start()
        else:

            def last_part(owner):
                return b.acc[:tok, lanes_of(owner)] + jnp.dot(
                    b.normed[:, :down_rows], b.wo[h, :, lanes_of(owner)],
                    preferred_element_type=f32,
                )

            with scope("emit2"):
                out_scatter.emit(last_part)
    with scope("middle2"):
        out_scatter.middle()
    with scope("result2"):
        top, low = out_scatter.result()
    half = tok // 2
    b.mid[:half, :] = (b.mid[:half, :].astype(f32) + top).astype(bf16)
    b.mid[half:, :] = (b.mid[half:, :].astype(f32) + low).astype(bf16)

    rows_gather.drain()

    step_rows = STEP_BLOCKS * cap
    steps = grp_count // STEP_BLOCKS
    def step_gather(step):
        def block(owner, half):
            return b.gathered.at[owner, pl.ds((STEP_BLOCKS * step + half) * cap, cap)]

        def whole(owner):
            return b.gathered.at[owner, pl.ds(step * step_rows, step_rows)]

        return gather(block, whole, b.g_send.at[step], b.g_recv.at[step])

    gathers = [step_gather(s) for s in range(steps)]
    own = pl.multiple_of(grp // per_owner * cap, cap)
    b.gathered[tp, 0:cap, :] = jnp.dot(
        b.select[pl.ds(own, cap), :], b.mid[...], preferred_element_type=f32
    ).astype(bf16)
    early = [gathers[0].own[0], gathers[0].own[3]] if square else []
    for copy in early:
        copy.start()
    for e in range(E_MLP):
        b.picked[e] = jnp.dot(
            b.select[e * cap : (e + 1) * cap, :], b.mid[...], preferred_element_type=f32
        ).astype(bf16)
    dispatch = []
    for i in range(1, grp_count):
        peer = (grp + grp_count - i) % grp_count
        copy = remote(
            b.picked.at[peer // per_owner], b.gathered.at[tp, pl.ds(i * cap, cap)],
            b.d_send.at[i - 1], b.d_recv.at[i - 1], {"grp": peer},
        )
        copy.start()
        dispatch.append(copy)
    scatters = [
        scatter(
            step_rows, (s % 2) * step_rows, b.po3.at[s], b.pi3.at[s], b.so3.at[s], b.si3.at[s],
            b.s3_send.at[s], b.s3_recv.at[s],
        )
        for s in range(steps)
    ]

    def pass_on(step):
        for i in range(step * STEP_BLOCKS, (step + 1) * STEP_BLOCKS):
            if i:
                dispatch[i - 1].wait_recv()
        for n, copy in enumerate(gathers[step].own):
            if step or not (square and n in (0, 3)):
                copy.start()

    ret = []

    def give_back(step):
        for q, value in enumerate(scatters[step].result()):
            i = step * STEP_BLOCKS + q
            back = pl.ds(pl.multiple_of(grp * cap, cap), cap)
            if i == 0:
                b.ret_in[back, :] = value.astype(bf16)
            else:
                b.ret_out[i * cap : (i + 1) * cap, :] = value.astype(bf16)
                copy = remote(
                    b.ret_out.at[pl.ds(i * cap, cap)], b.ret_in.at[back],
                    b.t_send.at[i - 1], b.t_recv.at[i - 1], {"grp": (grp + i) % grp_count},
                )
                copy.start()
                ret.append(copy)

    with scope("pass0"):
        pass_on(0)
    with scope("forward0"):
        gathers[0].forward()
    with scope("pass1"):
        pass_on(1)
    at_rounds("out")
    if steps > 2:
        with scope("pass2"):
            pass_on(2)
    for load in wide_loads + down_loads:
        load.wait()
    for step in range(steps):
        part = slice(step * step_rows, (step + 1) * step_rows)
        with scope(f"finish{step}"):
            gathers[step].finish()
        if step == 0 and steps > 1:
            with scope("forward1"):
                gathers[1].forward()
        square_sum = None
        for s in range(tp_count):
            block = b.gathered[s, part, :].astype(f32)
            term = jnp.sum(block * block, axis=-1, keepdims=True)
            square_sum = term if square_sum is None else square_sum + term
        factor = lax.rsqrt(square_sum * (1.0 / model) + epsilon)
        for s in range(tp_count):
            lanes = slice(s * width, (s + 1) * width)
            b.rows_all[:step_rows, lanes] = (
                b.gathered[s, part, :].astype(f32) * factor * gain_mlp[:, lanes]
            ).astype(bf16)
        xn = b.rows_all[:step_rows, :]
        wg = b.wg[...] if hasattr(b, "wg") else b.wide[:, :hid]
        wu = b.wu[...] if hasattr(b, "wu") else b.wide[:, hid : 2 * hid]
        gate = jnp.dot(xn, wg, preferred_element_type=f32)
        up = jnp.dot(xn, wu, preferred_element_type=f32)
        units = (gate / (1.0 + jnp.exp(-gate)) * up).astype(bf16)
        if step + 3 < steps:
            with scope(f"pass{step+3}"):
                pass_on(step + 3)
        if step + 2 < steps:
            with scope(f"forward{step+2}"):
                gathers[step + 2].forward()
        if step == 0:
            at_rounds("disp")
        elif step == 1:
            at_rounds("last")
        if step >= 1:
            with scope(f"mid{step-1}"):
                scatters[step - 1].middle()
        if step >= 2:
            with scope(f"give{step-2}"):
                give_back(step - 2)

        def down(owner):
            total = None
            for c, size in down_parts:
                term = jnp.dot(
                    units[:, c * down_rows : c * down_rows + size],
                    b.wo[c, :size, lanes_of(owner)], preferred_element_type=f32,
                )
                total = term if total is None else total + term
            return total

        with scope(f"emit3_{step}"):
            scatters[step].emit(down)
    if steps >= 2:
        with scope(f"give{steps-2}"):
            give_back(steps - 2)
    with scope(f"mid{steps-1}"):
        scatters[steps - 1].middle()
    with scope(f"give{steps-1}"):
        give_back(steps - 1)
    with scope("ret_wait"):
        for copy in ret:
            copy.wait_recv()
    hidden[...] = (
        b.mid[...].astype(f32)
        + lax.dot_general(
            b.mix[...], b.ret_in[...], (((0,), (0,)), ((), ())), preferred_element_type=f32
        )
    ).astype(bf16)
    with scope("page_wait"):
        for copy in page_copies:
            copy.wait()
    for copy in info_copies + dispatch + ret + [x for line in sides for x in line]:
        copy.wait_send()

    @pl.when(grp + 2 < grp_count)
    def _():
        for copy in first_hop + [x for line in rings for x in line]:
            copy.wait_send()

    for group in [out_scatter] + gathers + scatters:
        group.drain()


def place_kernel(slot_of, arrived, layer_out, placed, hidden_out, held, rows, isem, osem):
    groups, pair = arrived.shape[:2]
    reads = [
        pltpu.make_async_copy(
            arrived.at[i // pair, i % pair], held.at[i], isem.at[i]
        )
        for i in range(groups * pair)
    ]
    writes = [
        pltpu.make_async_copy(
            held.at[i], placed.at[slot_of[i // pair, 0, i % pair]], osem.at[i]
        )
        for i in range(groups * pair)
    ]
    reads.append(pltpu.make_async_copy(layer_out, rows, isem.at[groups * pair]))
    writes.append(pltpu.make_async_copy(rows, hidden_out, osem.at[groups * pair]))
    for copy in reads:
        copy.start()
    for read, write in zip(reads, writes):
        read.wait()
        write.start()
    for copy in writes:
        copy.wait()


def on_device(
    stream,
    lengths,
    att_routes,
    att_gate,
    mlp_routes,
    mlp_gate,
    gain_attn,
    gain_mlp,
    w_query,
    w_key,
    w_value,
    w_output,
    w_gate,
    w_up,
    w_down,
    cache_in,
    page_table,
):
    grp_count = lax.axis_size("grp")
    tp_count = lax.axis_size("tp")
    rows, model = stream.shape
    tok = rows * tp_count
    width = w_key.shape[1]
    heads = width // HD
    hid = w_gate.shape[1]
    pages_dev = page_table.shape[0]
    pair = pages_dev // grp_count
    dma = pltpu.SemaphoreType.DMA
    sds = jax.ShapeDtypeStruct
    vmem = pltpu.VMEM
    peers = tp_count - 1
    square = tp_count == 4
    cap = tok * TOPK * 5 // (E_MLP * 4)
    reach = grp_count // 2
    hops = reach // 2
    window = (reach + 1) * tok
    step_rows = STEP_BLOCKS * cap
    steps = grp_count // STEP_BLOCKS
    slots = grp_count * cap
    rounds = pair * PIECES

    frequency = rope_base ** (-(np.arange(HD // 2) * 2.0 / HD))
    freq = jnp.asarray(np.concatenate([frequency, frequency])[None, :], f32)
    page_len = tok // pages_dev
    piece = (page_len // PIECES * cache_in.shape[1] * cache_in.shape[2],) + cache_in.shape[3:]
    pages = cache_in.reshape((pages_dev, PIECES) + piece)

    scratch = {
        "held": vmem((pages_dev, PIECES) + piece, bf16),
        "staged": vmem((pair, PIECES, grp_count) + piece, bf16),
        "slot_out": vmem((grp_count, 1, META), jnp.int32),
        "wkv": vmem((model, 2 * width), bf16),
        "wo": vmem((heads, E_ATT * HD, model), bf16),
        "rows_all": vmem((max(tok, step_rows), model), bf16),
        "normed": vmem((tok, model), bf16),
        "info": vmem((tok, META), bf16),
        "cosine": vmem((tok, HD), f32),
        "sine": vmem((tok, HD), f32),
        "bias": vmem((tok, window), f32),
        "kv": vmem((heads, reach + 1, tok, 2 * HD), bf16),
        "query": vmem((TOPK, heads, tok, HD), bf16),
        "acc": vmem((max(tok, 2 * step_rows), model), f32),
        "mid": vmem((tok, width), bf16),
        "select": vmem((E_MLP * cap, tok), bf16),
        "mix": vmem((slots, tok), bf16),
        "picked": vmem((E_MLP, cap, width), bf16),
        "gathered": vmem((tp_count, slots, width), bf16),
        "ret_out": vmem((slots, width), bf16),
        "ret_in": vmem((slots, width), bf16),
        "page_sem": dma((1,)),
        "kv_sem": dma((2,)),
        "q_sem": dma((E_ATT,)),
        "o_sem": dma((heads, E_ATT)),
        "w_sem": dma((2 + heads,)),
        "row_send": dma((max(6, peers),)),
        "row_recv": dma((max(6, peers),)),
        "info_send": dma((peers,)),
        "info_recv": dma((peers,)),
        "self_sem": dma((rounds,)),
        "page_send": dma((rounds, grp_count - 1)),
        "page_recv": dma((rounds, grp_count - 1)),
        "slot_send": dma((grp_count - 1,)),
        "slot_recv": dma((grp_count - 1,)),
        "hop_send": dma((tp_count,)),
        "hop_recv": dma((tp_count,)),
        "ring_send": dma((heads, hops)),
        "ring_recv": dma((heads, hops)),
        "side_send": dma((heads, hops)),
        "side_recv": dma((heads, hops)),
        "s2_send": dma((max(6, peers),)),
        "s2_recv": dma((max(6, peers),)),
        "d_send": dma((grp_count - 1,)),
        "d_recv": dma((grp_count - 1,)),
        "g_send": dma((steps, max(6, peers))),
        "g_recv": dma((steps, max(6, peers))),
        "s3_send": dma((steps, max(6, peers))),
        "s3_recv": dma((steps, max(6, peers))),
        "t_send": dma((grp_count - 1,)),
        "t_recv": dma((grp_count - 1,)),
    }
    if hid % 128 == 0:
        scratch["wide"] = vmem((model, 2 * hid), bf16)
    else:
        scratch["wide"] = vmem((model, E_ATT * width), bf16)
        scratch["wg"] = vmem((model, hid), bf16)
        scratch["wu"] = vmem((model, hid), bf16)
    for stage, lead, count in (("2", (), tok), ("3", (steps,), step_rows)):
        if square:
            part, second = lead + (4, count // 2, width), lead + (2, count // 2, width)
        else:
            part, second = lead + (peers, count, width), lead + (1, 16, 128)
        scratch["po" + stage] = vmem(part, bf16)
        scratch["pi" + stage] = vmem(part, bf16)
        scratch["so" + stage] = vmem(second, bf16)
        scratch["si" + stage] = vmem(second, bf16)

    layer_out, arrived, slot_of = pl.pallas_call(
        functools.partial(layer_kernel, (tp_count, grp_count, cap), tuple(scratch)),
        out_shape=(
            sds((tok, width), bf16),
            sds((grp_count, pair, PIECES) + piece, bf16),
            sds((grp_count, 1, META), jnp.int32),
        ),
        in_specs=[SM] * 2 + [VM] * 8 + [ANY] * 8,
        out_specs=(VM, ANY, VM),
        scratch_shapes=list(scratch.values()),
        compiler_params=pltpu.CompilerParams(
            vmem_limit_bytes=VMEM_LIMIT, collective_id=1, has_side_effects=True
        ),
        name="layer",
    )(
        lengths, page_table, stream, att_routes.T, att_gate.T, mlp_routes.T, mlp_gate.T,
        gain_attn[None, :], gain_mlp[None, :], freq,
        w_query, w_key, w_value, w_output, w_gate, w_up, w_down, pages,
    )

    cache_out, hidden_out = pl.pallas_call(
        place_kernel,
        out_shape=(sds((pages_dev, PIECES) + piece, bf16), sds((tok, width), bf16)),
        in_specs=[SM, ANY, ANY],
        out_specs=(ANY, ANY),
        scratch_shapes=[
            vmem((pages_dev, PIECES) + piece, bf16),
            vmem((tok, width), bf16),
            dma((pages_dev + 1,)),
            dma((pages_dev + 1,)),
        ],
        compiler_params=pltpu.CompilerParams(vmem_limit_bytes=VMEM_LIMIT),
        name="place_pages",
    )(slot_of, arrived, layer_out)
    return (hidden_out, cache_out.reshape((pages_dev, page_len) + cache_in.shape[1:]))


def solution(mesh):
    return jax.shard_map(
        on_device,
        mesh=mesh,
        in_specs=(
            P(("grp", "tp"), None),
            P(),
            P(("grp", "tp"), None),
            P(("grp", "tp"), None),
            P(("grp", "tp"), None),
            P(("grp", "tp"), None),
            P(),
            P(),
            P(None, None, "tp"),
            P(None, "tp"),
            P(None, "tp"),
            P(None, "tp", None),
            P(None, ("grp", "tp")),
            P(None, ("grp", "tp")),
            P(("grp", "tp"), None),
            P("grp", None, None, "tp", None),
            P("grp"),
        ),
        out_specs=(P("grp", "tp"), P("grp", None, None, None, "tp", None)),
        check_vma=False,
    )
```
